128 devices in a mesh: sens: 4 (over y_hi, core), par: 32 (over y_lo, x, z).
Axes of the slice: x: 4, y: 4 (y_hi: 2, y_lo: 2; y = y_hi * 2 + y_lo), z: 4, core: 2. Of those that a mesh axis runs over, the one named last changes fastest.
Arguments:
- data: bfloat16 [32, 600, 420], P(None, 'sens'), may hold values from -6 to 6
- green: bfloat16 [64, 600, 2, 4096], P(None, 'sens', None, 'par'), may hold values from -0.1875 to 0.1875
- freqs: int32 [64], replicated, may hold values from 1 to 209, as said below
- sensor_order: int32 [600], P('sens'), may hold values from 0 to 599, each once
- kappa: float32 [32, 128], P('par'), may hold values from 0.05 to 0.5
- theta: float32 [32, 128], P('par'), may hold values from 0.5 to 2
Outputs:
- prior_field: bfloat16 [32, 420, 32, 128], P('sens', None, 'par')
The draws below stay inside these ranges and needn't reach their ends.
Inputs may be any that keep to these rules, and one draw needn't show every extreme that they name: `freqs`: distinct; both 1 and 209 appear. `sensor_order`: each sensor fills exactly one slot.
All inputs are finite; a program needn't handle non-finite values.
Results may differ from the reference program's by a relative error of at most 0.015.
Values may be sent and summed in bfloat16 or wider, within the bound.
No kernel may reach another device: no remote copies, remote signals or barrier semaphores. Data moves between devices by JAX's collectives and lax.ppermute only.
A program may use at most 64 MiB of HBM per device.

```python
import math
import jax
import jax.numpy as jnp
from jax import lax

S = 600
NT = 420
K = 64
COLS = 128
SWEEPS = 6
R = 32
ROWS = 32
P_SIZE = 4096
N_PAR = 32


def draw_freqs(key, part):
    shuffled = jax.random.permutation(key, NT // 2 - 3)[:K - 2] + 2
    ends = jnp.array([1, NT // 2 - 1], dtype=jnp.int32)
    return jnp.concatenate([ends, shuffled.astype(jnp.int32)])


def shard_levels(stream_key, extent, pieces, low, high):
    loudness = 1.0
    for dim, blocks in pieces:
        draws = jax.random.uniform(jax.random.fold_in(jax.random.fold_in(stream_key, 6), dim), (blocks,), jnp.float32, low / len(pieces), high / len(pieces))
        loudness = loudness * jnp.repeat(jnp.exp(draws), extent[dim] // blocks).reshape((-1,) + (1,) * (len(extent) - 1 - dim))
    return loudness


def noise(rng, extent, spread, bound, shards=(), kind=jnp.bfloat16):
    drawn = spread * jax.random.normal(rng, extent, jnp.float32)
    if shards:
        drawn = drawn * shard_levels(rng, extent, shards, -0.22, 0.18)
    return jnp.clip(drawn, -bound, bound).astype(kind)


def setup_inputs(seed: int = 0) -> dict:
    splits = jax.random.split(jax.random.key(seed), 7)
    data = noise(splits[0], (R, S, NT), 1.0, 6.0, ((1, 4),))
    green = noise(splits[1], (K, S, 2, P_SIZE), (2 * S) ** -0.5, 0.1875, ((1, 4), (3, 32)))
    freqs = draw_freqs(jax.random.fold_in(splits[6], 71), 0)
    sensor_order = jax.random.permutation(splits[3], S).astype(jnp.int32)
    kappa = jnp.clip(jnp.exp(math.log(0.5) - 2.3025851 * jax.random.uniform(splits[4], (ROWS, COLS), jnp.float32) ** shard_levels(splits[4], (ROWS, COLS), ((0, 32),), -0.2, 0.2)), 0.05, 0.5)
    theta = jnp.clip(jnp.exp(math.log(2.0) - 1.3862944 * jax.random.uniform(splits[5], (ROWS, COLS), jnp.float32) ** shard_levels(splits[5], (ROWS, COLS), ((0, 32),), -0.2, 0.2)), 0.5, 2.0)
    return dict(data=data, green=green, freqs=freqs, sensor_order=sensor_order, kappa=kappa, theta=theta)


lower_bound = 0.05
upper_bound = 16.5

def make_tables(freqs):
    times = jnp.arange(NT, dtype=jnp.int32)
    phase = times[:, None] * freqs[None, :] % NT
    angle = phase.astype(jnp.float32) * (2.0 * math.pi / NT)
    cosine = jnp.cos(angle)
    sine = jnp.sin(angle)
    forward = (jnp.concatenate([cosine, -sine], axis=1) / math.sqrt(NT)).astype(jnp.bfloat16)
    inverse = (jnp.concatenate([cosine, -sine], axis=1) / math.sqrt(K)).astype(jnp.bfloat16)
    return (forward, inverse)

def chebyshev_scalars():
    center = 0.5 * (upper_bound + lower_bound)
    radius = 0.5 * (upper_bound - lower_bound)
    alphas = []
    betas = []
    alpha = 1.0 / center
    for sweep_index in range(SWEEPS):
        if sweep_index == 0:
            alpha = 1.0 / center
            beta = 0.0
        else:
            if sweep_index == 1:
                beta = 0.5 * (radius * alpha) ** 2
            else:
                beta = (radius * alpha / 2.0) ** 2
            alpha = 1.0 / (center - beta / alpha)
        alphas.append(alpha)
        betas.append(beta)
    return (alphas, betas)

def face_terms(theta):
    padded = jnp.pad(theta, 1, mode='edge')
    north = 0.5 * (theta + padded[:-2, 1:-1])
    south = 0.5 * (theta + padded[2:, 1:-1])
    west = 0.5 * (theta + padded[1:-1, :-2])
    east = 0.5 * (theta + padded[1:-1, 2:])
    return (north, south, west, east)

def reference(data, green, freqs, sensor_order, kappa, theta):
    forward, inverse = make_tables(freqs)
    hp = lax.Precision.HIGHEST
    spectra = jnp.einsum('rst,tj->rsj', data.astype(jnp.float32), forward.astype(jnp.float32), precision=hp).astype(jnp.bfloat16)
    slotted = jnp.take(spectra, sensor_order, axis=1)

    def one_frequency(index):
        block = lax.dynamic_index_in_dim(green, index, 0, keepdims=False).astype(jnp.float32)
        real_data = lax.dynamic_index_in_dim(slotted, index, 2, keepdims=False).astype(jnp.float32)
        imag_data = lax.dynamic_index_in_dim(slotted, index + K, 2, keepdims=False).astype(jnp.float32)
        real_green = block[:, 0, :]
        imag_green = block[:, 1, :]
        real_part = jnp.dot(real_data, real_green, precision=hp) + jnp.dot(imag_data, imag_green, precision=hp)
        imag_part = jnp.dot(imag_data, real_green, precision=hp) - jnp.dot(real_data, imag_green, precision=hp)
        return (real_part, imag_part)
    real_all, imag_all = lax.map(one_frequency, jnp.arange(K, dtype=jnp.int32))
    adjoint = jnp.concatenate([jnp.transpose(real_all, (1, 0, 2)), jnp.transpose(imag_all, (1, 0, 2))], axis=1)
    adjoint_b = adjoint.astype(jnp.bfloat16)
    field = jnp.einsum('tj,rjp->rtp', inverse.astype(jnp.float32), adjoint_b.astype(jnp.float32), precision=hp)
    grid = field.reshape(R, NT, N_PAR, ROWS, COLS // N_PAR)
    grid = jnp.transpose(grid, (0, 1, 3, 4, 2)).reshape(R, NT, ROWS, COLS)
    north, south, west, east = face_terms(theta)
    diagonal = kappa + north + south + west + east

    def operator(field_in):
        padded = jnp.pad(field_in, ((0, 0), (0, 0), (1, 1), (1, 1)))
        return diagonal * field_in - north * padded[:, :, :-2, 1:-1] - south * padded[:, :, 2:, 1:-1] - west * padded[:, :, 1:-1, :-2] - east * padded[:, :, 1:-1, 2:]
    alphas, betas = chebyshev_scalars()
    solution = jnp.zeros_like(grid)
    residual = grid
    direction = grid
    for sweep_index in range(SWEEPS):
        if sweep_index == 0:
            direction = residual
        else:
            direction = residual + betas[sweep_index] * direction
        solution = solution + alphas[sweep_index] * direction
        if sweep_index + 1 < SWEEPS:
            residual = residual - alphas[sweep_index] * operator(direction)
    return solution.astype(jnp.bfloat16)
```

```python
import functools
import math

import jax
import jax.numpy as jnp
from jax import lax
from jax.experimental import pallas as pl
from jax.experimental.pallas import tpu as pltpu
from jax.sharding import PartitionSpec as P

NT = 420
K = 64
R = 32
ROWS = 32
COLS = 128
SWEEPS = 6
SENS = 4
PAR = 32
HERE = 150
PAD = 152
WINDOWS = (0, 128, 344, 472, 256)
BLOCK = 32 * len(WINDOWS)
SENT = BLOCK + 8
CHUNK = 25
AXES = ("sens", "par")
LOWER, UPPER = 0.05, 16.5
f32, bf16, i32 = jnp.float32, jnp.bfloat16, jnp.int32
VMEM = pl.BlockSpec(memory_space=pltpu.VMEM)
SMEM = pl.BlockSpec(memory_space=pltpu.SMEM)
HBM = pl.BlockSpec(memory_space=pltpu.HBM)
NT_DIMS = (((1,), (1,)), ((), ()))
TN_DIMS = (((0,), (0,)), ((), ()))


def iota(shape, dim):
    return lax.broadcasted_iota(i32, shape, dim)


def chebyshev_scalars():
    center = 0.5 * (UPPER + LOWER)
    radius = 0.5 * (UPPER - LOWER)
    alphas, betas = [1.0 / center], [0.0]
    for i in range(1, SWEEPS):
        beta = 0.5 * (radius * alphas[-1]) ** 2 if i == 1 else (radius * alphas[-1] / 2.0) ** 2
        alphas.append(1.0 / (center - beta / alphas[-1]))
        betas.append(beta)
    return alphas, betas


def wave(freq, imag, shape):
    t = iota(shape, 0).astype(f32)
    p = t * freq
    m = p - NT * jnp.floor(p * (1.0 / NT))
    m = jnp.where(m < 0, m + NT, m)
    m = jnp.where(m >= NT, m - NT, m)
    m = jnp.where(imag, m + NT // 4, m)
    m = jnp.where(m >= NT, m - NT, m)
    x = (NT // 4 - jnp.minimum(m, NT - m)) * (2.0 * math.pi / NT)
    x2 = x * x
    acc = -1.0 / math.factorial(11) + x2 * (1.0 / math.factorial(13))
    for n, sign in ((9, 1), (7, -1), (5, 1), (3, -1)):
        acc = sign / math.factorial(n) + x2 * acc
    return x + x * x2 * acc


def spectra_kernel(where_ref, freqs_hbm, data_ref, out_ref, buf, part, freqs_ref, sems):
    freqs_copy = pltpu.make_async_copy(freqs_hbm, freqs_ref, sems.at[HERE // CHUNK])
    freqs_copy.start()
    copies = []
    for n in range(HERE // CHUNK):
        at = pl.ds(n * CHUNK, CHUNK)
        copies.append(pltpu.make_async_copy(data_ref.at[at], buf.at[at], sems.at[n]))
        copies[-1].start()
    freqs_copy.wait()
    first = 2 * where_ref[0]
    lane = iota((NT, 128), 1)
    freq = jnp.where(lane < 64, freqs_ref[first], freqs_ref[first + 1]).astype(f32)
    table = (wave(freq, (lane & 32) != 0, (NT, 128)) * (1.0 / math.sqrt(NT))).astype(bf16)
    own = (iota((R, 128), 1) & 31) == iota((R, 128), 0)
    own = jnp.where(own, 1.0, 0.0).astype(f32).reshape(1, 4, 8, 128)
    for n in range(HERE // CHUNK):
        copies[n].wait()
        x = buf[n * CHUNK : (n + 1) * CHUNK].reshape(CHUNK * R, NT)
        y = jnp.dot(x, table, preferred_element_type=f32).reshape(CHUNK, 4, 8, 128)
        y = jnp.sum(y * own, axis=1).reshape(CHUNK * 8, 128)
        part[n * CHUNK * 8 : (n + 1) * CHUNK * 8, :] = y.astype(bf16)
    fold = (iota((PAD, HERE * 8), 1) >> 3) == iota((PAD, HERE * 8), 0)
    fold = jnp.where(fold, 1.0, 0.0).astype(bf16)
    out_ref[...] = jnp.dot(fold, part[...], preferred_element_type=f32).astype(bf16)


def split3(x):
    hi = x.astype(bf16).astype(f32)
    mid = (x - hi).astype(bf16).astype(f32)
    return hi, mid, x - hi - mid


def slots_kernel(where_ref, spectra_ref, order_ref, kappa_ref, theta_ref, out_ref):
    sens = where_ref[1]
    core = where_ref[2]
    order = order_ref[...]
    block = jnp.where(order >= 450, 3, jnp.where(order >= 300, 2, jnp.where(order >= 150, 1, 0)))
    row = (block ^ sens) * PAD + order - HERE * block
    pick = jnp.where(iota((SENS * PAD, HERE), 0) == row, 1.0, 0.0).astype(bf16)
    chosen = lax.dot_general(spectra_ref[...], pick, TN_DIMS, preferred_element_type=f32)
    width = 128 * len(WINDOWS)
    at = iota((HERE, width), 1)
    green_row = at
    for n, start in enumerate(WINDOWS):
        green_row = jnp.where((at >> 7) == n, start + (at & 127), green_row)
    slot = jnp.where(green_row >= 2 * HERE, green_row - 2 * HERE, green_row) >> 1
    shared_end = (at >= 4 * 128) & ((at & 127) >= WINDOWS[2] - WINDOWS[4])
    slot = jnp.where(shared_end, -1, slot)
    spread = jnp.where(slot == iota((HERE, width), 0), 1.0, 0.0).astype(bf16)
    wide = jnp.dot(chosen.astype(bf16), spread, preferred_element_type=f32)
    lane = iota((R, 128), 1)
    odd = (lane & 1) == 1
    rows = []
    for n in range(len(WINDOWS)):
        w = wide[:, n * 128 : (n + 1) * 128]
        first = jnp.where(odd, w[32:64], w[0:32])
        second = jnp.where(odd, w[96:128], w[64:96])
        if n < 2:
            v = first
        elif n < 4:
            v = second
        else:
            v = jnp.where(lane < 2 * HERE - WINDOWS[4], first, second)
        g0, g1, g2, g3 = v[0:8], v[8:16], v[16:24], v[24:32]
        mine = core == 0
        rows += [
            jnp.where(mine, g0, g1),
            jnp.where(mine, g2, g3),
            jnp.where(mine, g1, g0),
            jnp.where(mine, g3, g2),
        ]
    ka = split3(kappa_ref[...])
    th = split3(theta_ref[...])
    tail = jnp.zeros((8, 128), f32)
    line = iota((8, 128), 0)
    for n, v in enumerate(ka + th):
        tail = jnp.where(line == n, v, tail)
    block_out = jnp.concatenate(rows + [tail], axis=0).astype(bf16)
    for n in range(PAR):
        out_ref[n] = block_out


def prior_kernel(freqs_ref, tails_ref, coef_ref, itab_ref):
    flat = tails_ref[...].reshape(PAR * 8, 128)
    lane = iota((32, 128), 1)
    cell = iota((32, 128), 0)
    kappa = jnp.zeros((32, 128), f32)
    theta = jnp.zeros((32, 128), f32)
    src_row = iota((PAR * 8, 128), 0)
    to_lane = iota((PAR * 8, 128), 1)
    part = src_row & 7
    for q in range(4):
        pick = jnp.where(lane == q * 32 + cell, 1.0, 0.0).astype(bf16)
        turned = lax.dot_general(pick, flat, NT_DIMS, preferred_element_type=f32).astype(bf16)
        here = to_lane == 4 * (src_row >> 3) + q
        put = jnp.where(here & (part < 3), 1.0, 0.0).astype(bf16)
        kappa = kappa + jnp.dot(turned, put, preferred_element_type=f32)
        put = jnp.where(here & (part >= 3) & (part < 6), 1.0, 0.0).astype(bf16)
        theta = theta + jnp.dot(turned, put, preferred_element_type=f32)
    up, down = lane < 4, lane >= 124
    left = (cell == 0) & ((lane & 3) == 0)
    right = (cell == 31) & ((lane & 3) == 3)
    north = jnp.where(up, theta, pltpu.roll(theta, 4, 1))
    south = jnp.where(down, theta, pltpu.roll(theta, 124, 1))
    back = pltpu.roll(theta, 1, 0)
    west = jnp.where(cell == 0, pltpu.roll(back, 1, 1), back)
    west = jnp.where(left, theta, west)
    ahead = pltpu.roll(theta, 31, 0)
    east = jnp.where(cell == 31, pltpu.roll(ahead, 127, 1), ahead)
    east = jnp.where(right, theta, east)
    north, south, west, east = (0.5 * (theta + v) for v in (north, south, west, east))
    coef_ref[0] = kappa + north + south + west + east
    coef_ref[1] = jnp.where(up, 0.0, north)
    coef_ref[2] = jnp.where(down, 0.0, south)
    coef_ref[3] = jnp.where(left, 0.0, west)
    coef_ref[4] = jnp.where(right, 0.0, east)
    twice = jnp.where((iota((K, 128), 1) >> 1) == iota((K, 128), 0), 1.0, 0.0).astype(bf16)
    freqs = jnp.broadcast_to(freqs_ref[...].astype(f32), (8, K)).astype(bf16)
    freq = jnp.dot(freqs, twice, preferred_element_type=f32)[0:1]
    imag = (iota((NT, 128), 1) & 1) == 1
    itab_ref[...] = (wave(freq, imag, (NT, 128)) * (1.0 / math.sqrt(K))).astype(bf16)


def product_kernel(left_ref, green_ref, keep_ref, send_ref, turned_ref):
    a, b = iota((128, 128), 0), iota((128, 128), 1)
    turn = jnp.where((a ^ 1) == b, jnp.where((a & 1) == 1, 1.0, -1.0), 0.0).astype(bf16)
    is_first = iota((R, 128), 1) < 2 * HERE - WINDOWS[4]
    zero = jnp.zeros((R, 128), bf16)

    @pl.loop(0, PAR // 8)
    def _(m):
        for u in range(8):
            x = jnp.dot(left_ref[8 * m + u, 0:BLOCK, :], turn, preferred_element_type=f32)
            turned_ref[8 * m + u] = x.astype(bf16)

    def pair(i, base):
        def part(n, ref):
            return ref[i, n * 32 : (n + 1) * 32, :]

        def both(n, ref):
            return jnp.concatenate([part(n, ref), part(n + 1, ref)], axis=1)

        def green(start, count):
            return green_ref[pl.ds(base + start, count), :]

        first = jnp.concatenate([both(0, left_ref), both(0, turned_ref)], axis=0)
        second = jnp.concatenate([both(2, left_ref), both(2, turned_ref)], axis=0)
        s, st = part(4, left_ref), part(4, turned_ref)
        shared = [jnp.where(is_first, v, zero) for v in (s, st)]
        shared += [jnp.where(is_first, zero, v) for v in (s, st)]
        shared = jnp.concatenate(shared, axis=0)
        edge = jnp.dot(shared, green(WINDOWS[4], 128), preferred_element_type=f32)
        one = jnp.dot(first, green(WINDOWS[0], 256), preferred_element_type=f32) + edge[0:64]
        two = jnp.dot(second, green(WINDOWS[2], 256), preferred_element_type=f32) + edge[64:128]
        x = (one[0:32], one[32:64], two[0:32], two[32:64])
        for half, ref in ((0, keep_ref), (1, send_ref)):
            for yh in range(2):
                at = half * 16 + yh * 8
                v = jnp.concatenate([g[at : at + 8] for g in x], axis=0)
                ref[yh, i] = v.astype(bf16)

    @pl.loop(0, PAR // 8)
    def _(m):
        for u in range(8):
            pair(8 * m + u, pl.multiple_of(m * 4800, 16) + 600 * u)


def smooth_kernel(moved_ref, coef_ref, out_ref, dirn, res, sol, turned):
    alphas, betas = chebyshev_scalars()

    def start(b, _):
        v = moved_ref[b].astype(f32) + moved_ref[PAR + b].astype(f32)
        dirn[0, b + 1] = v.astype(bf16).astype(f32)
        return 0

    lax.fori_loop(0, PAR, start, 0, unroll=4)

    def halo(slot):
        dirn[slot, 0] = pltpu.roll(dirn[slot, PAR], 1, 1)
        dirn[slot, PAR + 1] = pltpu.roll(dirn[slot, 1], 127, 1)

    for i in range(SWEEPS - 1):
        now, later = i % 2, (i + 1) % 2
        halo(now)

        def sweep(b, _, i=i, now=now, later=later):
            def coef(n):
                return coef_ref[n, pl.ds(b, 1), :]

            u = dirn[now, b + 1]
            au = coef(0) * u
            au = au - coef(1) * pltpu.roll(u, 4, 1)
            au = au - coef(2) * pltpu.roll(u, 124, 1)
            au = au - coef(3) * dirn[now, b]
            au = au - coef(4) * dirn[now, b + 2]
            at = pl.ds(pl.multiple_of(b * 32, 32), 32)
            r = (u if i == 0 else res[at, :]) - alphas[i] * au
            x = alphas[0] * u if i == 0 else sol[at, :]
            d = r + betas[i + 1] * u
            sol[at, :] = x + alphas[i + 1] * d
            if i < SWEEPS - 2:
                res[at, :] = r
                dirn[later, b + 1] = d
            return 0

        lax.fori_loop(0, PAR, sweep, 0, unroll=4)
    lane = iota((32, 128), 1)
    gather = jnp.where((lane >> 2) == iota((32, 128), 0), 1.0, 0.0).astype(bf16)
    for f in range(32):
        x = sol[pl.ds(f, 32, stride=32), :]
        b = [jnp.where((lane & 3) == q, x, 0.0) for q in range(4)]
        b = jnp.concatenate(b, axis=0).astype(bf16)
        y = lax.dot_general(gather, b, NT_DIMS, preferred_element_type=f32)
        turned[pl.ds(f, 32, stride=32), :] = y
    out_ref[...] = turned[...].astype(bf16).reshape(ROWS, 32, 128)


def inverse_kernel(back_ref, itab_ref, out_ref, wide, mixed):
    wide[...] = back_ref[...].reshape(PAR * 32, 128).astype(f32)
    itab = itab_ref[...]
    for r in range(8):
        x = wide[pl.ds(r, 128, stride=8), :].astype(bf16)
        mixed[pl.ds(r, NT, stride=8), :] = jnp.dot(itab, x, preferred_element_type=f32)
    out_ref[...] = mixed[...].astype(bf16).reshape(NT, 8, 128)


def call(kernel, out, in_specs, scratch=(), mib=8):
    many = isinstance(out, (tuple, list))
    return pl.pallas_call(
        kernel,
        out_shape=out,
        in_specs=in_specs,
        out_specs=[VMEM] * len(out) if many else VMEM,
        scratch_shapes=list(scratch),
        compiler_params=pltpu.CompilerParams(vmem_limit_bytes=mib << 20),
    )


def shape(*dims, dtype=bf16):
    return jax.ShapeDtypeStruct(dims, dtype)


def partner(bit):
    return [(s * PAR + b, (s ^ bit) * PAR + b) for s in range(SENS) for b in range(PAR)]


def local(data, green, freqs, sensor_order, kappa, theta):
    sens, par = lax.axis_index("sens"), lax.axis_index("par")
    place = jnp.stack([par, sens, sens & 1]).astype(i32)
    spectra = call(
        spectra_kernel,
        shape(PAD, 128),
        [SMEM, HBM, HBM],
        [
            pltpu.VMEM((HERE, R, NT), bf16),
            pltpu.VMEM((HERE * 8, 128), bf16),
            pltpu.SMEM((K,), i32),
            pltpu.SemaphoreType.DMA((HERE // CHUNK + 1,)),
        ],
        mib=56,
    )(place, freqs, jnp.transpose(data, (1, 0, 2)))
    chip = jnp.concatenate([spectra, lax.ppermute(spectra, AXES, partner(1))], axis=0)
    every = jnp.concatenate([chip, lax.ppermute(chip, AXES, partner(2))], axis=0)
    sent = call(slots_kernel, shape(PAR, SENT, 128), [SMEM, VMEM, VMEM, VMEM, VMEM])(
        place, every, sensor_order.reshape(1, HERE), kappa, theta
    )
    left = lax.all_to_all(sent, "par", 0, 0, tiled=True)
    coef, itab = call(
        prior_kernel, [shape(5, 32, 128, dtype=f32), shape(NT, 128)], [VMEM, VMEM]
    )(freqs.reshape(1, K), left[:, BLOCK:, :])
    keep, send = call(
        product_kernel,
        [shape(2, PAR, 32, 128)] * 2,
        [VMEM, VMEM],
        [pltpu.VMEM((PAR, BLOCK, 128), bf16)],
    )(left, green.reshape(K * HERE * 2, 128))
    other = lax.ppermute(send, AXES, partner(1))
    keep, coef, itab = lax.optimization_barrier((keep, coef, itab))
    summed = (keep.astype(f32) + other.astype(f32)).astype(bf16).reshape(2 * PAR, 32, 128)
    groups = [[(2 * y + c) * PAR + b for y in range(2) for b in range(PAR)] for c in range(2)]
    moved = lax.all_to_all(summed, AXES, 0, 0, tiled=True, axis_index_groups=groups)
    smooth = call(
        smooth_kernel,
        shape(ROWS, 32, 128),
        [VMEM, VMEM],
        [
            pltpu.VMEM((2, PAR + 2, 32, 128), f32),
            pltpu.VMEM((PAR * 32, 128), f32),
            pltpu.VMEM((PAR * 32, 128), f32),
            pltpu.VMEM((PAR * 32, 128), f32),
        ],
    )(moved, coef)
    back = lax.all_to_all(smooth, "par", 0, 0, tiled=True)
    out = call(
        inverse_kernel,
        shape(NT, 8, 128),
        [VMEM, VMEM],
        [pltpu.VMEM((PAR * 32, 128), f32), pltpu.VMEM((NT * 8, 128), f32)],
    )(back, itab)
    return jnp.transpose(out, (1, 0, 2)).reshape(8, NT, 1, 128)


def solution(mesh):
    placed = (
        P(None, "sens", None),
        P(None, "sens", None, "par"),
        P(),
        P("sens"),
        P("par", None),
        P("par", None),
    )
    return jax.shard_map(
        local, mesh=mesh, in_specs=placed, out_specs=P("sens", None, "par", None), check_vma=False
    )
```

```python
import functools
import math

import jax
import jax.numpy as jnp
from jax import lax
from jax.experimental import pallas as pl
from jax.experimental.pallas import tpu as pltpu
from jax.sharding import PartitionSpec as P

NT = 420
K = 64
R = 32
ROWS = 32
COLS = 128
SWEEPS = 6
SENS = 4
PAR = 32
HERE = 150
PAD = 152
WINDOWS = (0, 128, 344, 472, 256)
BLOCK = 32 * len(WINDOWS)
CHUNK = 40
UNROLL = 16
PIECES = -(-HERE // CHUNK)
AXES = ("sens", "par")
LOWER, UPPER = 0.05, 16.5
f32, bf16, i32 = jnp.float32, jnp.bfloat16, jnp.int32
VMEM = pl.BlockSpec(memory_space=pltpu.VMEM)
SMEM = pl.BlockSpec(memory_space=pltpu.SMEM)
HBM = pl.BlockSpec(memory_space=pltpu.HBM)
NT_DIMS = (((1,), (1,)), ((), ()))
TN_DIMS = (((0,), (0,)), ((), ()))


def iota(shape, dim):
    return lax.broadcasted_iota(i32, shape, dim)


def chebyshev_series():
    d, c = 0.5 * (UPPER + LOWER), 0.5 * (UPPER - LOWER)
    values = []
    for m in range(SWEEPS):
        lam = d - c * math.cos(math.pi * (m + 0.5) / SWEEPS)
        x, res, dirn, alpha = 0.0, 1.0, 0.0, 1.0 / d
        for i in range(SWEEPS):
            beta = 0.0
            if i > 0:
                beta = 0.5 * (c * alpha) ** 2 if i == 1 else (c * alpha / 2.0) ** 2
                alpha = 1.0 / (d - beta / alpha)
            dirn = res + beta * dirn
            x = x + alpha * dirn
            res = res - alpha * lam * dirn
        values.append(x)
    series = [
        2.0 / SWEEPS * sum(v * math.cos(k * math.pi * (m + 0.5) / SWEEPS) for m, v in enumerate(values))
        for k in range(SWEEPS)
    ]
    return [0.5 * series[0]] + series[1:]


def wave(freq, imag, shape, dim):
    t = iota(shape, dim).astype(f32)
    p = t * freq
    m = p - NT * jnp.floor(p * (1.0 / NT))
    m = jnp.where(m < 0, m + NT, m)
    m = jnp.where(m >= NT, m - NT, m)
    m = jnp.where(imag, m + NT // 4, m)
    m = jnp.where(m >= NT, m - NT, m)
    x = (NT // 4 - jnp.minimum(m, NT - m)) * (2.0 * math.pi / NT)
    x2 = x * x
    acc = -1.0 / math.factorial(11) + x2 * (1.0 / math.factorial(13))
    for n, sign in ((9, 1), (7, -1), (5, 1), (3, -1)):
        acc = sign / math.factorial(n) + x2 * acc
    return x + x * x2 * acc


def spectra_kernel(freqs_hbm, data_ref, out_ref, buf, freqs_ref, sems):
    freqs_copy = pltpu.make_async_copy(freqs_hbm, freqs_ref, sems.at[PIECES])
    freqs_copy.start()
    copies = []
    for n in range(PIECES):
        at = pl.ds(n * CHUNK, min(CHUNK, HERE - n * CHUNK))
        copies.append(pltpu.make_async_copy(data_ref.at[at], buf.at[at], sems.at[n]))
        copies[-1].start()
    freqs_copy.wait()
    first = 2 * lax.axis_index("par")
    line = iota((8, NT), 0)
    freq = jnp.where(line < 2, freqs_ref[first], freqs_ref[first + 1]).astype(f32)
    table = wave(freq, (line & 1) == 1, (8, NT), 1) * (1.0 / math.sqrt(NT))
    table = [jnp.broadcast_to(table[j : j + 1], (R, NT)) for j in range(4)]
    table = jnp.concatenate(table, axis=0).astype(bf16)
    own = (iota((R, 128), 1) & 31) == iota((R, 128), 0)
    own = jnp.where(own, 1.0, 0.0).astype(f32).reshape(1, 4, 8, 128)
    fold = (iota((CHUNK, CHUNK * 8), 1) >> 3) == iota((CHUNK, CHUNK * 8), 0)
    fold = jnp.where(fold, 1.0, 0.0).astype(bf16)
    for n, copy in enumerate(copies):
        copy.wait()
        count = min(CHUNK, HERE - n * CHUNK)
        parts = []
        for start in range(0, count, count // 2):
            at = n * CHUNK + start
            x = buf[at : at + count // 2].reshape(count // 2 * R, NT)
            y = lax.dot_general(x, table, NT_DIMS, preferred_element_type=f32)
            y = jnp.sum(y.reshape(count // 2, 4, 8, 128) * own, axis=1)
            parts.append(y.reshape(count // 2 * 8, 128))
        y = jnp.concatenate(parts, axis=0).astype(bf16)
        rows = -(-count // 8) * 8
        y = jnp.dot(fold[:rows, : count * 8], y, preferred_element_type=f32)
        out_ref[n * CHUNK : n * CHUNK + rows, :] = y.astype(bf16)


def split3(x):
    hi = x.astype(bf16).astype(f32)
    mid = (x - hi).astype(bf16).astype(f32)
    return hi, mid, x - hi - mid


def slots_kernel(own_ref, core_ref, far_ref, last_ref, order_ref, kappa_ref, theta_ref, out_ref):
    sens = lax.axis_index("sens")
    core = sens & 1
    order = order_ref[...]
    block = jnp.where(order >= 450, 3, jnp.where(order >= 300, 2, jnp.where(order >= 150, 1, 0)))
    row = (block ^ sens) * PAD + order - HERE * block
    pick = jnp.where(iota((SENS * PAD, HERE), 0) == row, 1.0, 0.0).astype(bf16)
    every = [ref[...] for ref in (own_ref, core_ref, far_ref, last_ref)]
    every = jnp.concatenate(every, axis=0)
    chosen = lax.dot_general(every, pick, TN_DIMS, preferred_element_type=f32)
    width = 128 * len(WINDOWS)
    at = iota((HERE, width), 1)
    green_row = at
    for n, start in enumerate(WINDOWS):
        green_row = jnp.where((at >> 7) == n, start + (at & 127), green_row)
    slot = jnp.where(green_row >= 2 * HERE, green_row - 2 * HERE, green_row) >> 1
    shared_end = (at >= 4 * 128) & ((at & 127) >= WINDOWS[2] - WINDOWS[4])
    slot = jnp.where(shared_end, -1, slot)
    spread = jnp.where(slot == iota((HERE, width), 0), 1.0, 0.0).astype(bf16)
    wide = jnp.dot(chosen.astype(bf16), spread, preferred_element_type=f32)
    lane = iota((R, 128), 1)
    odd = (lane & 1) == 1
    parts = jnp.zeros((8, 128), f32)
    for n, v in enumerate(split3(kappa_ref[...]) + split3(theta_ref[...])):
        parts = jnp.where(iota((8, 128), 0) == n, v, parts)
    turns = [parts if q == 3 else pltpu.roll(parts, 96 - 32 * q, 1) for q in range(4)]
    mine = core == 0
    tails = [jnp.where(mine, turns[a], turns[b]) for a, b in ((0, 2), (2, 0), (1, 3), (3, 1))]
    tails = jnp.concatenate(tails, axis=0)
    rows = []
    for n in range(len(WINDOWS)):
        w = wide[:, n * 128 : (n + 1) * 128]
        first = jnp.where(odd, w[32:64], w[0:32])
        second = jnp.where(odd, w[96:128], w[64:96])
        if n < 2:
            v = first
        elif n < 4:
            v = second
        else:
            v = jnp.where(lane < 2 * HERE - WINDOWS[4], first, second)
            v = jnp.where(lane < 96, v, tails)
        g0, g1, g2, g3 = v[0:8], v[8:16], v[16:24], v[24:32]
        rows += [
            jnp.where(mine, g0, g1),
            jnp.where(mine, g2, g3),
            jnp.where(mine, g1, g0),
            jnp.where(mine, g3, g2),
        ]
    block_out = jnp.concatenate(rows, axis=0).astype(bf16)
    for n in range(PAR):
        out_ref[n] = block_out


def prior_kernel(freqs_ref, left_ref, coef_ref, itab_ref, gather_ref):
    flat = left_ref[:, BLOCK - 32 :, :].reshape(PAR * 32, 128)
    lane = iota((32, 128), 1)
    cell = iota((32, 128), 0)
    pick = jnp.where(lane == 96 + cell, 1.0, 0.0).astype(bf16)
    turned = lax.dot_general(pick, flat, NT_DIMS, preferred_element_type=f32).astype(bf16)
    row, to = iota((PAR * 32, 128), 0), iota((PAR * 32, 128), 1)
    here = to == 4 * (row >> 5) + ((row >> 3) & 3)
    part = row & 7
    put = jnp.where(here & (part < 3), 1.0, 0.0).astype(bf16)
    kappa = jnp.dot(turned, put, preferred_element_type=f32)
    put = jnp.where(here & (part >= 3) & (part < 6), 1.0, 0.0).astype(bf16)
    theta = jnp.dot(turned, put, preferred_element_type=f32)
    up, down = lane < 4, lane >= 124
    left = (cell == 0) & ((lane & 3) == 0)
    right = (cell == 31) & ((lane & 3) == 3)
    north = jnp.where(up, theta, pltpu.roll(theta, 4, 1))
    south = jnp.where(down, theta, pltpu.roll(theta, 124, 1))
    back = pltpu.roll(theta, 1, 0)
    west = jnp.where(cell == 0, pltpu.roll(back, 1, 1), back)
    west = jnp.where(left, theta, west)
    ahead = pltpu.roll(theta, 31, 0)
    east = jnp.where(cell == 31, pltpu.roll(ahead, 127, 1), ahead)
    east = jnp.where(right, theta, east)
    north, south, west, east = (0.5 * (theta + v) for v in (north, south, west, east))
    d, c = 0.5 * (UPPER + LOWER), 0.5 * (UPPER - LOWER)
    coefs = [
        (2.0 / c) * (d - (kappa + north + south + west + east)),
        jnp.where(up, 0.0, (2.0 / c) * north),
        jnp.where(down, 0.0, (2.0 / c) * south),
        jnp.where(left, 0.0, (2.0 / c) * west),
        jnp.where(right, 0.0, (2.0 / c) * east),
    ]
    for n, v in enumerate(coefs):
        coef_ref[n] = jnp.broadcast_to(v.reshape(32, 1, 128), (32, 8, 128))
    m, n = iota((256, 1024), 0), iota((256, 1024), 1)
    same = ((m & 7) == (n >> 7)) & ((m >> 3) == ((n & 127) >> 2))
    gather_ref[...] = jnp.where(same, 1.0, 0.0).astype(bf16)
    twice = jnp.where((iota((K, 128), 1) >> 1) == iota((K, 128), 0), 1.0, 0.0).astype(bf16)
    freqs = jnp.broadcast_to(freqs_ref[...].astype(f32), (8, K)).astype(bf16)
    freq = jnp.dot(freqs, twice, preferred_element_type=f32)[0:1]
    imag = (iota((NT, 128), 1) & 1) == 1
    itab_ref[...] = (wave(freq, imag, (NT, 128), 0) * (1.0 / math.sqrt(K))).astype(bf16)


def fetch_kernel(green_hbm, out_ref, sems):
    rows = K * HERE * 2 // 4
    copies = []
    for n in range(4):
        at = pl.ds(n * rows, rows)
        copies.append(pltpu.make_async_copy(green_hbm.at[at], out_ref.at[at], sems.at[n]))
        copies[-1].start()
    for copy in copies:
        copy.wait()


def product_kernel(left_ref, green_ref, keep_ref, send_ref, turned_ref):
    a, b = iota((128, 128), 0), iota((128, 128), 1)
    turn = jnp.where((a ^ 1) == b, jnp.where((a & 1) == 1, 1.0, -1.0), 0.0).astype(bf16)
    shared_lane = iota((R, 128), 1)
    is_first = shared_lane < 2 * HERE - WINDOWS[4]
    is_second = (shared_lane >= 2 * HERE - WINDOWS[4]) & (shared_lane < WINDOWS[2] - WINDOWS[4])
    zero = jnp.zeros((R, 128), bf16)

    @pl.loop(0, PAR // 8)
    def _(m):
        for u in range(8):
            x = jnp.dot(left_ref[8 * m + u], turn, preferred_element_type=f32)
            turned_ref[8 * m + u] = x.astype(bf16)

    def pair(i, base):
        def part(n, ref):
            return ref[i, n * 32 : (n + 1) * 32, :]

        def both(n, ref):
            return jnp.concatenate([part(n, ref), part(n + 1, ref)], axis=1)

        def green(start, count):
            return green_ref[pl.ds(base + start, count), :]

        first = jnp.concatenate([both(0, left_ref), both(0, turned_ref)], axis=0)
        second = jnp.concatenate([both(2, left_ref), both(2, turned_ref)], axis=0)
        s, st = part(4, left_ref), part(4, turned_ref)
        shared = [jnp.where(is_first, v, zero) for v in (s, st)]
        shared += [jnp.where(is_second, v, zero) for v in (s, st)]
        shared = jnp.concatenate(shared, axis=0)
        edge = jnp.dot(shared, green(WINDOWS[4], 128), preferred_element_type=f32)
        one = jnp.dot(first, green(WINDOWS[0], 256), preferred_element_type=f32) + edge[0:64]
        two = jnp.dot(second, green(WINDOWS[2], 256), preferred_element_type=f32) + edge[64:128]
        x = (one[0:32], one[32:64], two[0:32], two[32:64])
        for half, ref in ((0, keep_ref), (1, send_ref)):
            for yh in range(2):
                at = half * 16 + yh * 8
                v = jnp.concatenate([g[at : at + 8] for g in x], axis=0)
                ref[yh, i] = v.astype(bf16)

    @pl.loop(0, PAR // 8)
    def _(m):
        for u in range(8):
            pair(8 * m + u, pl.multiple_of(m * 4800, 16) + 600 * u)


def smooth_kernel(moved_ref, coef_ref, gather_ref, out_ref, both, grid, sol):
    series = chebyshev_series()
    below = (iota((256, 128), 0) & 127) == iota((256, 128), 1) + 4
    below = jnp.where(below, 1.0, 0.0).astype(bf16)

    def start(b, _):
        v = moved_ref[b].astype(f32) + moved_ref[PAR + b].astype(f32)
        v = v.astype(bf16).astype(f32).reshape(4, 8, 128)
        grid[b] = v
        both[0, b + 1] = series[5] * v
        return 0

    lax.fori_loop(0, PAR, start, 0, unroll=4)

    def halo(slot):
        both[slot, 0] = pltpu.roll(both[slot, PAR], 1, 2)
        both[slot, PAR + 1] = pltpu.roll(both[slot, 1], 127, 2)

    for k in range(4, -1, -1):
        now, later = k % 2, (k + 1) % 2
        halo(now)

        def step(b, _, k=k, now=now, later=later):
            def coef(n):
                return coef_ref[n, b]

            u = both[now, b + 1]
            v = coef(0) * u
            v = v + coef(1) * pltpu.roll(u, 4, 2)
            hi = u.reshape(32, 128).astype(bf16)
            lo = (u.reshape(32, 128) - hi.astype(f32)).astype(bf16)
            south = jnp.concatenate([hi, lo], axis=1)
            south = jnp.dot(south, below, preferred_element_type=f32)
            v = v + coef(2) * south.reshape(4, 8, 128)
            v = v + coef(3) * both[now, b]
            v = v + coef(4) * both[now, b + 2]
            if k == 0:
                v = 0.5 * v
            v = v + series[k] * grid[b]
            if k < 4:
                v = v - both[later, b + 1]
            if k == 0:
                sol[pl.ds(pl.multiple_of(b * 32, 32), 32), :] = v.reshape(32, 128)
            else:
                both[later, b + 1] = v
            return 0

        lax.fori_loop(0, PAR, step, 0, unroll=UNROLL)
    quarter = iota((32, 128), 1) & 3
    for pair in (0, 16):
        turned = []
        for f in range(8):
            column = []
            for g in (pair, pair + 8):
                x = sol[pl.ds(g + f, 32, stride=32), :]
                column += [jnp.where(quarter == q, x, 0.0).astype(bf16) for q in range(4)]
            turned.append(jnp.concatenate(column, axis=0))
        turned = jnp.concatenate(turned, axis=1)
        y = lax.dot_general(gather_ref[...], turned, NT_DIMS, preferred_element_type=f32)
        for n, g in enumerate((pair, pair + 8)):
            v = y[:, n * 128 : (n + 1) * 128].reshape(ROWS, 8, 128)
            out_ref[:, g : g + 8, :] = v.astype(bf16)


def inverse_kernel(back_ref, itab_ref, out_hbm, wide, mixed, ready, sems):
    wide[...] = back_ref[...].reshape(PAR * 32, 128).astype(f32)
    xs = [wide[pl.ds(r, 128, stride=8), :].astype(bf16) for r in range(8)]
    copies = []
    for n, (start, count) in enumerate(((0, 144), (144, 144), (288, 132))):
        at = pl.ds(start, count)
        itab = itab_ref[at, :]
        for r in range(8):
            y = jnp.dot(itab, xs[r], preferred_element_type=f32)
            mixed[pl.ds(8 * start + r, count, stride=8), :] = y
        y = mixed[8 * start : 8 * (start + count), :].astype(bf16)
        ready[at] = y.reshape(count, 8, 128)
        copies.append(pltpu.make_async_copy(ready.at[at], out_hbm.at[at], sems.at[n]))
        copies[-1].start()
    for copy in copies:
        copy.wait()


def call(kernel, out, in_specs, scratch=(), mib=8, to=VMEM):
    many = isinstance(out, (tuple, list))
    return pl.pallas_call(
        kernel,
        out_shape=out,
        in_specs=in_specs,
        out_specs=[to] * len(out) if many else to,
        scratch_shapes=list(scratch),
        compiler_params=pltpu.CompilerParams(vmem_limit_bytes=mib << 20),
    )


def shape(*dims, dtype=bf16):
    return jax.ShapeDtypeStruct(dims, dtype)


def in_hbm(x):
    return pltpu.with_memory_space_constraint(x, pltpu.HBM)


def partner(bit):
    return [(s * PAR + b, (s ^ bit) * PAR + b) for s in range(SENS) for b in range(PAR)]


def local(data, green, freqs, sensor_order, kappa, theta):
    spectra = call(
        spectra_kernel,
        shape(PAD, 128),
        [HBM, HBM],
        [
            pltpu.VMEM((HERE, R, NT), bf16),
            pltpu.SMEM((K,), i32),
            pltpu.SemaphoreType.DMA((PIECES + 1,)),
        ],
        mib=52,
    )(in_hbm(freqs), in_hbm(jnp.transpose(data, (1, 0, 2))))
    far = lax.ppermute(spectra, AXES, partner(2))
    near = lax.ppermute(spectra, AXES, partner(1))
    green, _ = lax.optimization_barrier((green, spectra))
    green = call(
        fetch_kernel, shape(K * HERE * 2, 128), [HBM], [pltpu.SemaphoreType.DMA((4,))]
    )(in_hbm(green.reshape(K * HERE * 2, 128)))
    far, near, green = lax.optimization_barrier((far, near, green))
    last = lax.ppermute(far, AXES, partner(1))
    sent = call(slots_kernel, shape(PAR, BLOCK, 128), [VMEM] * 7)(
        spectra, near, far, last, sensor_order.reshape(1, HERE), kappa, theta
    )
    left = lax.all_to_all(sent, "par", 0, 0, tiled=True)
    coef, itab, gather = call(
        prior_kernel,
        [shape(5, 32, 8, 128, dtype=f32), shape(NT, 128), shape(256, 1024)],
        [VMEM, VMEM],
    )(freqs.reshape(1, K), left)
    keep, send = call(
        product_kernel,
        [shape(2, PAR, 32, 128)] * 2,
        [VMEM, VMEM],
        [pltpu.VMEM((PAR, BLOCK, 128), bf16)],
    )(left, green)
    other = lax.ppermute(send, AXES, partner(1))
    keep, coef, itab, gather = lax.optimization_barrier((keep, coef, itab, gather))
    summed = (keep.astype(f32) + other.astype(f32)).astype(bf16).reshape(2 * PAR, 32, 128)
    groups = [[(2 * y + c) * PAR + b for y in range(2) for b in range(PAR)] for c in range(2)]
    moved = lax.all_to_all(summed, AXES, 0, 0, tiled=True, axis_index_groups=groups)
    smooth = call(
        smooth_kernel,
        shape(ROWS, 32, 128),
        [VMEM] * 3,
        [
            pltpu.VMEM((2, PAR + 2, 4, 8, 128), f32),
            pltpu.VMEM((PAR, 4, 8, 128), f32),
            pltpu.VMEM((PAR * 32, 128), f32),
        ],
    )(moved, coef, gather)
    back = lax.all_to_all(smooth, "par", 0, 0, tiled=True)
    out = call(
        inverse_kernel,
        shape(NT, 8, 128),
        [VMEM, VMEM],
        [
            pltpu.VMEM((PAR * 32, 128), f32),
            pltpu.VMEM((NT * 8, 128), f32),
            pltpu.VMEM((NT, 8, 128), bf16),
            pltpu.SemaphoreType.DMA((3,)),
        ],
        to=HBM,
    )(back, itab)
    return jnp.transpose(out, (1, 0, 2)).reshape(8, NT, 1, 128)


def solution(mesh):
    placed = (
        P(None, "sens", None),
        P(None, "sens", None, "par"),
        P(),
        P("sens"),
        P("par", None),
        P("par", None),
    )
    return jax.shard_map(
        local, mesh=mesh, in_specs=placed, out_specs=P("sens", None, "par", None), check_vma=False
    )
```

```python
import math

import jax
import jax.numpy as jnp
from jax import lax
from jax.experimental import pallas as pl
from jax.experimental.pallas import tpu as pltpu
from jax.sharding import PartitionSpec as P

NT = 420
K = 64
R = 32
ROWS = 32
SWEEPS = 6
SENS = 4
PAR = 32
HERE = 150
PAD = 152
WINDOWS = (0, 128, 344, 472, 256)
BLOCK = 32 * len(WINDOWS)
CHUNK = 80
UNROLL = 16
PIECES = -(-HERE // CHUNK)
AXES = ("sens", "par")
LOWER, UPPER = 0.05, 16.5
f32, bf16, i32 = jnp.float32, jnp.bfloat16, jnp.int32
VMEM = pl.BlockSpec(memory_space=pltpu.VMEM)
SMEM = pl.BlockSpec(memory_space=pltpu.SMEM)
HBM = pl.BlockSpec(memory_space=pltpu.HBM)
NT_DIMS = (((1,), (1,)), ((), ()))
TN_DIMS = (((0,), (0,)), ((), ()))


def iota(shape, dim):
    return lax.broadcasted_iota(i32, shape, dim)


def chebyshev_series():
    d, c = 0.5 * (UPPER + LOWER), 0.5 * (UPPER - LOWER)
    values = []
    for m in range(SWEEPS):
        lam = d - c * math.cos(math.pi * (m + 0.5) / SWEEPS)
        x, res, dirn, alpha = 0.0, 1.0, 0.0, 1.0 / d
        for i in range(SWEEPS):
            beta = 0.0
            if i > 0:
                beta = 0.5 * (c * alpha) ** 2 if i == 1 else (c * alpha / 2.0) ** 2
                alpha = 1.0 / (d - beta / alpha)
            dirn = res + beta * dirn
            x = x + alpha * dirn
            res = res - alpha * lam * dirn
        values.append(x)
    series = [
        2.0 / SWEEPS * sum(v * math.cos(k * math.pi * (m + 0.5) / SWEEPS) for m, v in enumerate(values))
        for k in range(SWEEPS)
    ]
    return [0.5 * series[0]] + series[1:]


def wave(freq, imag, shape, dim):
    t = iota(shape, dim).astype(f32)
    p = t * freq
    m = p - NT * jnp.floor(p * (1.0 / NT))
    m = jnp.where(m < 0, m + NT, m)
    m = jnp.where(m >= NT, m - NT, m)
    m = jnp.where(imag, m + NT // 4, m)
    m = jnp.where(m >= NT, m - NT, m)
    x = (NT // 4 - jnp.minimum(m, NT - m)) * (2.0 * math.pi / NT)
    x2 = x * x
    acc = -1.0 / math.factorial(11) + x2 * (1.0 / math.factorial(13))
    for n, sign in ((9, 1), (7, -1), (5, 1), (3, -1)):
        acc = sign / math.factorial(n) + x2 * acc
    return x + x * x2 * acc


def spectra_kernel(freqs_hbm, data_ref, out_ref, buf, freqs_ref, sems):
    freqs_copy = pltpu.make_async_copy(freqs_hbm, freqs_ref, sems.at[PIECES])
    freqs_copy.start()
    copies = []
    for n in range(PIECES):
        at = pl.ds(n * CHUNK, min(CHUNK, HERE - n * CHUNK))
        copies.append(pltpu.make_async_copy(data_ref.at[at], buf.at[at], sems.at[n]))
        copies[-1].start()
    freqs_copy.wait()
    first = 2 * lax.axis_index("par")
    line = iota((8, NT), 0)
    freq = jnp.where(line < 2, freqs_ref[first], freqs_ref[first + 1]).astype(f32)
    table = wave(freq, (line & 1) == 1, (8, NT), 1) * (1.0 / math.sqrt(NT))
    table = [jnp.broadcast_to(table[j : j + 1], (R, NT)) for j in range(4)]
    table = jnp.concatenate(table, axis=0).astype(bf16)
    own = (iota((R, 128), 1) & 31) == iota((R, 128), 0)
    own = jnp.where(own, 1.0, 0.0).astype(f32).reshape(1, 4, 8, 128)
    fold = (iota((CHUNK, CHUNK * 8), 1) >> 3) == iota((CHUNK, CHUNK * 8), 0)
    fold = jnp.where(fold, 1.0, 0.0).astype(bf16)
    for n, copy in enumerate(copies):
        copy.wait()
        count = min(CHUNK, HERE - n * CHUNK)
        parts = []
        for start in range(0, count, count // 2):
            at = n * CHUNK + start
            x = buf[at : at + count // 2].reshape(count // 2 * R, NT)
            y = lax.dot_general(x, table, NT_DIMS, preferred_element_type=f32)
            y = jnp.sum(y.reshape(count // 2, 4, 8, 128) * own, axis=1)
            parts.append(y.reshape(count // 2 * 8, 128))
        y = jnp.concatenate(parts, axis=0).astype(bf16)
        rows = -(-count // 8) * 8
        y = jnp.dot(fold[:rows, : count * 8], y, preferred_element_type=f32)
        out_ref[n * CHUNK : n * CHUNK + rows, :] = y.astype(bf16)


def split3(x):
    hi = x.astype(bf16).astype(f32)
    mid = (x - hi).astype(bf16).astype(f32)
    return hi, mid, x - hi - mid


def slots_kernel(own_ref, core_ref, far_ref, last_ref, order_ref, kappa_ref, theta_ref, out_ref):
    sens = lax.axis_index("sens")
    core = sens & 1
    order = order_ref[...]
    block = jnp.where(order >= 450, 3, jnp.where(order >= 300, 2, jnp.where(order >= 150, 1, 0)))
    row = (block ^ sens) * PAD + order - HERE * block
    pick = jnp.where(iota((SENS * PAD, HERE), 0) == row, 1.0, 0.0).astype(bf16)
    every = [ref[...] for ref in (own_ref, core_ref, far_ref, last_ref)]
    every = jnp.concatenate(every, axis=0)
    chosen = lax.dot_general(every, pick, TN_DIMS, preferred_element_type=f32)
    width = 128 * len(WINDOWS)
    at = iota((HERE, width), 1)
    green_row = at
    for n, start in enumerate(WINDOWS):
        green_row = jnp.where((at >> 7) == n, start + (at & 127), green_row)
    slot = jnp.where(green_row >= 2 * HERE, green_row - 2 * HERE, green_row) >> 1
    shared_end = (at >= 4 * 128) & ((at & 127) >= WINDOWS[2] - WINDOWS[4])
    slot = jnp.where(shared_end, -1, slot)
    spread = jnp.where(slot == iota((HERE, width), 0), 1.0, 0.0).astype(bf16)
    wide = jnp.dot(chosen.astype(bf16), spread, preferred_element_type=f32)
    lane = iota((R, 128), 1)
    odd = (lane & 1) == 1
    parts = jnp.zeros((8, 128), f32)
    for n, v in enumerate(split3(kappa_ref[...]) + split3(theta_ref[...])):
        parts = jnp.where(iota((8, 128), 0) == n, v, parts)
    turns = [parts if q == 3 else pltpu.roll(parts, 96 - 32 * q, 1) for q in range(4)]
    mine = core == 0
    tails = [jnp.where(mine, turns[a], turns[b]) for a, b in ((0, 2), (2, 0), (1, 3), (3, 1))]
    tails = jnp.concatenate(tails, axis=0)
    rows = []
    for n in range(len(WINDOWS)):
        w = wide[:, n * 128 : (n + 1) * 128]
        first = jnp.where(odd, w[32:64], w[0:32])
        second = jnp.where(odd, w[96:128], w[64:96])
        if n < 2:
            v = first
        elif n < 4:
            v = second
        else:
            v = jnp.where(lane < 2 * HERE - WINDOWS[4], first, second)
            v = jnp.where(lane < 96, v, tails)
        g0, g1, g2, g3 = v[0:8], v[8:16], v[16:24], v[24:32]
        rows += [
            jnp.where(mine, g0, g1),
            jnp.where(mine, g2, g3),
            jnp.where(mine, g1, g0),
            jnp.where(mine, g3, g2),
        ]
    block_out = jnp.concatenate(rows, axis=0).astype(bf16)
    for n in range(PAR):
        out_ref[n] = block_out


def prior_kernel(freqs_ref, left_ref, coef_ref, itab_ref, gather_ref):
    flat = left_ref[:, BLOCK - 32 :, :].reshape(PAR * 32, 128)
    lane = iota((32, 128), 1)
    cell = iota((32, 128), 0)
    pick = jnp.where(lane == 96 + cell, 1.0, 0.0).astype(bf16)
    turned = lax.dot_general(pick, flat, NT_DIMS, preferred_element_type=f32).astype(bf16)
    row, to = iota((PAR * 32, 128), 0), iota((PAR * 32, 128), 1)
    here = to == 4 * (row >> 5) + ((row >> 3) & 3)
    part = row & 7
    put = jnp.where(here & (part < 3), 1.0, 0.0).astype(bf16)
    kappa = jnp.dot(turned, put, preferred_element_type=f32)
    put = jnp.where(here & (part >= 3) & (part < 6), 1.0, 0.0).astype(bf16)
    theta = jnp.dot(turned, put, preferred_element_type=f32)
    up, down = lane < 4, lane >= 124
    left = (cell == 0) & ((lane & 3) == 0)
    right = (cell == 31) & ((lane & 3) == 3)
    north = jnp.where(up, theta, pltpu.roll(theta, 4, 1))
    south = jnp.where(down, theta, pltpu.roll(theta, 124, 1))
    back = pltpu.roll(theta, 1, 0)
    west = jnp.where(cell == 0, pltpu.roll(back, 1, 1), back)
    west = jnp.where(left, theta, west)
    ahead = pltpu.roll(theta, 31, 0)
    east = jnp.where(cell == 31, pltpu.roll(ahead, 127, 1), ahead)
    east = jnp.where(right, theta, east)
    north, south, west, east = (0.5 * (theta + v) for v in (north, south, west, east))
    d, c = 0.5 * (UPPER + LOWER), 0.5 * (UPPER - LOWER)
    coefs = [
        (2.0 / c) * (d - (kappa + north + south + west + east)),
        jnp.where(up, 0.0, (2.0 / c) * north),
        jnp.where(down, 0.0, (2.0 / c) * south),
        jnp.where(left, 0.0, (2.0 / c) * west),
        jnp.where(right, 0.0, (2.0 / c) * east),
    ]
    for n, v in enumerate(coefs):
        coef_ref[n] = jnp.broadcast_to(v.reshape(32, 1, 128), (32, 8, 128))
    m, n = iota((256, 1024), 0), iota((256, 1024), 1)
    same = ((m & 7) == (n >> 7)) & ((m >> 3) == ((n & 127) >> 2))
    gather_ref[...] = jnp.where(same, 1.0, 0.0).astype(bf16)
    twice = jnp.where((iota((K, 128), 1) >> 1) == iota((K, 128), 0), 1.0, 0.0).astype(bf16)
    freqs = jnp.broadcast_to(freqs_ref[...].astype(f32), (8, K)).astype(bf16)
    freq = jnp.dot(freqs, twice, preferred_element_type=f32)[0:1]
    imag = (iota((NT, 128), 1) & 1) == 1
    itab_ref[...] = (wave(freq, imag, (NT, 128), 0) * (1.0 / math.sqrt(K))).astype(bf16)


def fetch_kernel(green_hbm, out_ref, sems):
    rows = K * HERE * 2 // 4
    copies = []
    for n in range(4):
        at = pl.ds(n * rows, rows)
        copies.append(pltpu.make_async_copy(green_hbm.at[at], out_ref.at[at], sems.at[n]))
        copies[-1].start()
    for copy in copies:
        copy.wait()


def product_kernel(left_ref, green_ref, keep_ref, send_ref, turned_ref):
    a, b = iota((128, 128), 0), iota((128, 128), 1)
    turn = jnp.where((a ^ 1) == b, jnp.where((a & 1) == 1, 1.0, -1.0), 0.0).astype(bf16)
    shared_lane = iota((R, 128), 1)
    is_first = shared_lane < 2 * HERE - WINDOWS[4]
    is_second = (shared_lane >= 2 * HERE - WINDOWS[4]) & (shared_lane < WINDOWS[2] - WINDOWS[4])
    zero = jnp.zeros((R, 128), bf16)

    @pl.loop(0, PAR // 8)
    def _(m):
        for u in range(8):
            x = jnp.dot(left_ref[8 * m + u], turn, preferred_element_type=f32)
            turned_ref[8 * m + u] = x.astype(bf16)

    def pair(i, base):
        def part(n, ref):
            return ref[i, n * 32 : (n + 1) * 32, :]

        def both(n, ref):
            return jnp.concatenate([part(n, ref), part(n + 1, ref)], axis=1)

        def green(start, count):
            return green_ref[pl.ds(base + start, count), :]

        first = jnp.concatenate([both(0, left_ref), both(0, turned_ref)], axis=0)
        second = jnp.concatenate([both(2, left_ref), both(2, turned_ref)], axis=0)
        s, st = part(4, left_ref), part(4, turned_ref)
        shared = [jnp.where(is_first, v, zero) for v in (s, st)]
        shared += [jnp.where(is_second, v, zero) for v in (s, st)]
        shared = jnp.concatenate(shared, axis=0)
        edge = jnp.dot(shared, green(WINDOWS[4], 128), preferred_element_type=f32)
        one = jnp.dot(first, green(WINDOWS[0], 256), preferred_element_type=f32) + edge[0:64]
        two = jnp.dot(second, green(WINDOWS[2], 256), preferred_element_type=f32) + edge[64:128]
        x = (one[0:32], one[32:64], two[0:32], two[32:64])
        for half, ref in ((0, keep_ref), (1, send_ref)):
            for yh in range(2):
                at = half * 16 + yh * 8
                v = jnp.concatenate([g[at : at + 8] for g in x], axis=0)
                ref[yh, i] = v.astype(bf16)

    @pl.loop(0, PAR // 8)
    def _(m):
        for u in range(8):
            pair(8 * m + u, pl.multiple_of(m * 4800, 16) + 600 * u)


def smooth_kernel(moved_ref, coef_ref, gather_ref, out_ref, both, grid, sol):
    series = chebyshev_series()

    def start(b, _):
        v = moved_ref[b].astype(f32) + moved_ref[PAR + b].astype(f32)
        v = v.astype(bf16).astype(f32).reshape(4, 8, 128)
        grid[b] = v
        both[0, b + 1] = series[5] * v
        return 0

    lax.fori_loop(0, PAR, start, 0, unroll=4)

    def halo(slot):
        both[slot, 0] = pltpu.roll(both[slot, PAR], 1, 2)
        both[slot, PAR + 1] = pltpu.roll(both[slot, 1], 127, 2)

    for k in range(4, -1, -1):
        now, later = k % 2, (k + 1) % 2
        halo(now)

        def step(b, _, k=k, now=now, later=later):
            def coef(n):
                return coef_ref[n, b]

            u = both[now, b + 1]
            v = coef(0) * u
            v = v + coef(1) * pltpu.roll(u, 4, 2)
            v = v + coef(2) * pltpu.roll(u, 124, 2)
            v = v + coef(3) * both[now, b]
            v = v + coef(4) * both[now, b + 2]
            if k == 0:
                v = 0.5 * v
            v = v + series[k] * grid[b]
            if k < 4:
                v = v - both[later, b + 1]
            if k == 0:
                sol[pl.ds(pl.multiple_of(b * 32, 32), 32), :] = v.reshape(32, 128)
            else:
                both[later, b + 1] = v
            return 0

        lax.fori_loop(0, PAR, step, 0, unroll=UNROLL)
    quarter = iota((32, 128), 1) & 3
    for pair in (0, 16):
        turned = []
        for f in range(8):
            column = []
            for g in (pair, pair + 8):
                x = sol[pl.ds(g + f, 32, stride=32), :]
                column += [jnp.where(quarter == q, x, 0.0).astype(bf16) for q in range(4)]
            turned.append(jnp.concatenate(column, axis=0))
        turned = jnp.concatenate(turned, axis=1)
        y = lax.dot_general(gather_ref[...], turned, NT_DIMS, preferred_element_type=f32)
        for n, g in enumerate((pair, pair + 8)):
            v = y[:, n * 128 : (n + 1) * 128].reshape(ROWS, 8, 128)
            out_ref[:, g : g + 8, :] = v.astype(bf16)


def inverse_kernel(back_ref, itab_ref, out_hbm, wide, mixed, ready, sems):
    wide[...] = back_ref[...].reshape(PAR * 32, 128).astype(f32)
    xs = [wide[pl.ds(r, 128, stride=8), :].astype(bf16) for r in range(8)]
    copies = []
    for n, (start, count) in enumerate(((0, 144), (144, 144), (288, 132))):
        at = pl.ds(start, count)
        itab = itab_ref[at, :]
        for r in range(8):
            y = jnp.dot(itab, xs[r], preferred_element_type=f32)
            mixed[pl.ds(8 * start + r, count, stride=8), :] = y
        y = mixed[8 * start : 8 * (start + count), :].astype(bf16)
        ready[at] = y.reshape(count, 8, 128)
        copies.append(pltpu.make_async_copy(ready.at[at], out_hbm.at[at], sems.at[n]))
        copies[-1].start()
    for copy in copies:
        copy.wait()


def call(kernel, out, in_specs, scratch=(), mib=8, to=VMEM):
    many = isinstance(out, (tuple, list))
    return pl.pallas_call(
        kernel,
        out_shape=out,
        in_specs=in_specs,
        out_specs=[to] * len(out) if many else to,
        scratch_shapes=list(scratch),
        compiler_params=pltpu.CompilerParams(vmem_limit_bytes=mib << 20),
    )


def shape(*dims, dtype=bf16):
    return jax.ShapeDtypeStruct(dims, dtype)


def in_hbm(x):
    return pltpu.with_memory_space_constraint(x, pltpu.HBM)


def partner(bit):
    return [(s * PAR + b, (s ^ bit) * PAR + b) for s in range(SENS) for b in range(PAR)]


def local(data, green, freqs, sensor_order, kappa, theta):
    spectra = call(
        spectra_kernel,
        shape(PAD, 128),
        [HBM, HBM],
        [
            pltpu.VMEM((HERE, R, NT), bf16),
            pltpu.SMEM((K,), i32),
            pltpu.SemaphoreType.DMA((PIECES + 1,)),
        ],
        mib=52,
    )(in_hbm(freqs), in_hbm(jnp.transpose(data, (1, 0, 2))))
    far = lax.ppermute(spectra, AXES, partner(2))
    near = lax.ppermute(spectra, AXES, partner(1))
    green, _ = lax.optimization_barrier((green, spectra))
    green = call(
        fetch_kernel, shape(K * HERE * 2, 128), [HBM], [pltpu.SemaphoreType.DMA((4,))]
    )(in_hbm(green.reshape(K * HERE * 2, 128)))
    far, near, green = lax.optimization_barrier((far, near, green))
    last = lax.ppermute(far, AXES, partner(1))
    sent = call(slots_kernel, shape(PAR, BLOCK, 128), [VMEM] * 7)(
        spectra, near, far, last, sensor_order.reshape(1, HERE), kappa, theta
    )
    left = lax.all_to_all(sent, "par", 0, 0, tiled=True)
    coef, itab, gather = call(
        prior_kernel,
        [shape(5, 32, 8, 128, dtype=f32), shape(NT, 128), shape(256, 1024)],
        [VMEM, VMEM],
    )(freqs.reshape(1, K), left)
    keep, send = call(
        product_kernel,
        [shape(2, PAR, 32, 128)] * 2,
        [VMEM, VMEM],
        [pltpu.VMEM((PAR, BLOCK, 128), bf16)],
    )(left, green)
    other = lax.ppermute(send, AXES, partner(1))
    keep, coef, itab, gather = lax.optimization_barrier((keep, coef, itab, gather))
    summed = (keep.astype(f32) + other.astype(f32)).astype(bf16).reshape(2 * PAR, 32, 128)
    groups = [[(2 * y + c) * PAR + b for y in range(2) for b in range(PAR)] for c in range(2)]
    moved = lax.all_to_all(summed, AXES, 0, 0, tiled=True, axis_index_groups=groups)
    smooth = call(
        smooth_kernel,
        shape(ROWS, 32, 128),
        [VMEM] * 3,
        [
            pltpu.VMEM((2, PAR + 2, 4, 8, 128), f32),
            pltpu.VMEM((PAR, 4, 8, 128), f32),
            pltpu.VMEM((PAR * 32, 128), f32),
        ],
    )(moved, coef, gather)
    back = lax.all_to_all(smooth, "par", 0, 0, tiled=True)
    out = call(
        inverse_kernel,
        shape(NT, 8, 128),
        [VMEM, VMEM],
        [
            pltpu.VMEM((PAR * 32, 128), f32),
            pltpu.VMEM((NT * 8, 128), f32),
            pltpu.VMEM((NT, 8, 128), bf16),
            pltpu.SemaphoreType.DMA((3,)),
        ],
        to=HBM,
    )(back, itab)
    return jnp.transpose(out, (1, 0, 2)).reshape(8, NT, 1, 128)


def solution(mesh):
    placed = (
        P(None, "sens", None),
        P(None, "sens", None, "par"),
        P(),
        P("sens"),
        P("par", None),
        P("par", None),
    )
    return jax.shard_map(
        local, mesh=mesh, in_specs=placed, out_specs=P("sens", None, "par", None), check_vma=False
    )
```

```python
import math

import jax
import jax.numpy as jnp
from jax import lax
from jax.experimental import pallas as pl
from jax.experimental.pallas import tpu as pltpu
from jax.sharding import PartitionSpec as P

NT = 420
K = 64
R = 32
ROWS = 32
SWEEPS = 6
SENS = 4
PAR = 32
HERE = 150
PAD = 152
WINDOWS = (0, 128, 344, 472, 256)
BLOCK = 32 * len(WINDOWS)
CHUNK = 80
UNROLL = 16
PIECES = -(-HERE // CHUNK)
AXES = ("sens", "par")
LOWER, UPPER = 0.05, 16.5
f32, bf16, i32 = jnp.float32, jnp.bfloat16, jnp.int32
VMEM = pl.BlockSpec(memory_space=pltpu.VMEM)
SMEM = pl.BlockSpec(memory_space=pltpu.SMEM)
HBM = pl.BlockSpec(memory_space=pltpu.HBM)
NT_DIMS = (((1,), (1,)), ((), ()))
TN_DIMS = (((0,), (0,)), ((), ()))


def iota(shape, dim):
    return lax.broadcasted_iota(i32, shape, dim)


def chebyshev_series():
    d, c = 0.5 * (UPPER + LOWER), 0.5 * (UPPER - LOWER)
    values = []
    for m in range(SWEEPS):
        lam = d - c * math.cos(math.pi * (m + 0.5) / SWEEPS)
        x, res, dirn, alpha = 0.0, 1.0, 0.0, 1.0 / d
        for i in range(SWEEPS):
            beta = 0.0
            if i > 0:
                beta = 0.5 * (c * alpha) ** 2 if i == 1 else (c * alpha / 2.0) ** 2
                alpha = 1.0 / (d - beta / alpha)
            dirn = res + beta * dirn
            x = x + alpha * dirn
            res = res - alpha * lam * dirn
        values.append(x)
    series = [
        2.0 / SWEEPS * sum(v * math.cos(k * math.pi * (m + 0.5) / SWEEPS) for m, v in enumerate(values))
        for k in range(SWEEPS)
    ]
    return [0.5 * series[0]] + series[1:]


def wave(freq, imag, shape, dim):
    t = iota(shape, dim).astype(f32)
    p = t * freq
    m = p - NT * jnp.floor(p * (1.0 / NT))
    m = jnp.where(m < 0, m + NT, m)
    m = jnp.where(m >= NT, m - NT, m)
    m = jnp.where(imag, m + NT // 4, m)
    m = jnp.where(m >= NT, m - NT, m)
    x = (NT // 4 - jnp.minimum(m, NT - m)) * (2.0 * math.pi / NT)
    x2 = x * x
    acc = -1.0 / math.factorial(11) + x2 * (1.0 / math.factorial(13))
    for n, sign in ((9, 1), (7, -1), (5, 1), (3, -1)):
        acc = sign / math.factorial(n) + x2 * acc
    return x + x * x2 * acc


def spectra_kernel(freqs_hbm, data_ref, out_ref, buf, freqs_ref, sems):
    freqs_copy = pltpu.make_async_copy(freqs_hbm, freqs_ref, sems.at[PIECES])
    freqs_copy.start()
    copies = []
    for n in range(PIECES):
        at = pl.ds(n * CHUNK, min(CHUNK, HERE - n * CHUNK))
        copies.append(pltpu.make_async_copy(data_ref.at[at], buf.at[at], sems.at[n]))
        copies[-1].start()
    freqs_copy.wait()
    first = 2 * lax.axis_index("par")
    line = iota((8, NT), 0)
    freq = jnp.where(line < 2, freqs_ref[first], freqs_ref[first + 1]).astype(f32)
    table = wave(freq, (line & 1) == 1, (8, NT), 1) * (1.0 / math.sqrt(NT))
    table = [jnp.broadcast_to(table[j : j + 1], (R, NT)) for j in range(4)]
    table = jnp.concatenate(table, axis=0).astype(bf16)
    own = (iota((R, 128), 1) & 31) == iota((R, 128), 0)
    own = jnp.where(own, 1.0, 0.0).astype(f32).reshape(1, 4, 8, 128)
    fold = (iota((CHUNK, CHUNK * 8), 1) >> 3) == iota((CHUNK, CHUNK * 8), 0)
    fold = jnp.where(fold, 1.0, 0.0).astype(bf16)
    for n, copy in enumerate(copies):
        copy.wait()
        count = min(CHUNK, HERE - n * CHUNK)
        parts = []
        for start in range(0, count, count // 2):
            at = n * CHUNK + start
            x = buf[at : at + count // 2].reshape(count // 2 * R, NT)
            y = lax.dot_general(x, table, NT_DIMS, preferred_element_type=f32)
            y = jnp.sum(y.reshape(count // 2, 4, 8, 128) * own, axis=1)
            parts.append(y.reshape(count // 2 * 8, 128))
        y = jnp.concatenate(parts, axis=0).astype(bf16)
        rows = -(-count // 8) * 8
        y = jnp.dot(fold[:rows, : count * 8], y, preferred_element_type=f32)
        out_ref[n * CHUNK : n * CHUNK + rows, :] = y.astype(bf16)


def split3(x):
    hi = x.astype(bf16).astype(f32)
    mid = (x - hi).astype(bf16).astype(f32)
    return hi, mid, x - hi - mid


def slots_kernel(
    own_ref, core_ref, far_ref, last_ref, order_ref, other_ref, kappa_ref, theta_ref, out_ref
):
    sens = lax.axis_index("sens")
    every = [ref[...] for ref in (own_ref, core_ref, far_ref, last_ref)]
    every = jnp.concatenate(every, axis=0)
    width = 128 * len(WINDOWS)
    at = iota((HERE, width), 1)
    green_row = at
    for n, start in enumerate(WINDOWS):
        green_row = jnp.where((at >> 7) == n, start + (at & 127), green_row)
    slot = jnp.where(green_row >= 2 * HERE, green_row - 2 * HERE, green_row) >> 1
    shared_end = (at >= 4 * 128) & ((at & 127) >= WINDOWS[2] - WINDOWS[4])
    slot = jnp.where(shared_end, -1, slot)
    spread = jnp.where(slot == iota((HERE, width), 0), 1.0, 0.0).astype(bf16)
    lane = iota((R, 128), 1)
    odd = (lane & 1) == 1

    def windows(order):
        block = jnp.where(order >= 150, 1, 0)
        block = jnp.where(order >= 300, 2, block)
        block = jnp.where(order >= 450, 3, block)
        row = (block ^ sens) * PAD + order - HERE * block
        pick = jnp.where(iota((SENS * PAD, HERE), 0) == row, 1.0, 0.0).astype(bf16)
        chosen = lax.dot_general(every, pick, TN_DIMS, preferred_element_type=f32)
        wide = jnp.dot(chosen.astype(bf16), spread, preferred_element_type=f32)
        for n in range(len(WINDOWS)):
            w = wide[:, n * 128 : (n + 1) * 128]
            first = jnp.where(odd, w[32:64], w[0:32])
            second = jnp.where(odd, w[96:128], w[64:96])
            if n < 2:
                v = first
            elif n < 4:
                v = second
            else:
                v = jnp.where(lane < 2 * HERE - WINDOWS[4], first, second)
            zero = (sens & 1) == 0
            yield [jnp.where(zero, v[y : y + 8], v[y + 8 : y + 16]) for y in (0, 16)]

    parts = jnp.zeros((8, 128), f32)
    for n, v in enumerate(split3(kappa_ref[...]) + split3(theta_ref[...])):
        parts = jnp.where(iota((8, 128), 0) == n, v, parts)
    turns = [parts if q == 3 else pltpu.roll(parts, 96 - 32 * q, 1) for q in range(4)]
    rows = []
    for one, two in zip(windows(order_ref[...]), windows(other_ref[...])):
        rows += one + two
    low = iota((8, 128), 1) < 96
    for q in range(4):
        rows[16 + q] = jnp.where(low, rows[16 + q], turns[q])
    block_out = jnp.concatenate(rows, axis=0).astype(bf16)
    for n in range(PAR):
        out_ref[n] = block_out


def prior_kernel(freqs_ref, left_ref, coef_ref, itab_ref, gather_ref):
    flat = left_ref[:, BLOCK - 32 :, :].reshape(PAR * 32, 128)
    lane = iota((32, 128), 1)
    cell = iota((32, 128), 0)
    pick = jnp.where(lane == 96 + cell, 1.0, 0.0).astype(bf16)
    turned = lax.dot_general(pick, flat, NT_DIMS, preferred_element_type=f32).astype(bf16)
    row, to = iota((PAR * 32, 128), 0), iota((PAR * 32, 128), 1)
    here = to == 4 * (row >> 5) + ((row >> 3) & 3)
    part = row & 7
    put = jnp.where(here & (part < 3), 1.0, 0.0).astype(bf16)
    kappa = jnp.dot(turned, put, preferred_element_type=f32)
    put = jnp.where(here & (part >= 3) & (part < 6), 1.0, 0.0).astype(bf16)
    theta = jnp.dot(turned, put, preferred_element_type=f32)
    up, down = lane < 4, lane >= 124
    left = (cell == 0) & ((lane & 3) == 0)
    right = (cell == 31) & ((lane & 3) == 3)
    north = jnp.where(up, theta, pltpu.roll(theta, 4, 1))
    south = jnp.where(down, theta, pltpu.roll(theta, 124, 1))
    back = pltpu.roll(theta, 1, 0)
    west = jnp.where(cell == 0, pltpu.roll(back, 1, 1), back)
    west = jnp.where(left, theta, west)
    ahead = pltpu.roll(theta, 31, 0)
    east = jnp.where(cell == 31, pltpu.roll(ahead, 127, 1), ahead)
    east = jnp.where(right, theta, east)
    north, south, west, east = (0.5 * (theta + v) for v in (north, south, west, east))
    d, c = 0.5 * (UPPER + LOWER), 0.5 * (UPPER - LOWER)
    coefs = [
        (2.0 / c) * (d - (kappa + north + south + west + east)),
        jnp.where(up, 0.0, (2.0 / c) * north),
        jnp.where(down, 0.0, (2.0 / c) * south),
        jnp.where(left, 0.0, (2.0 / c) * west),
        jnp.where(right, 0.0, (2.0 / c) * east),
    ]
    for n, v in enumerate(coefs):
        coef_ref[n] = jnp.broadcast_to(v.reshape(32, 1, 128), (32, 8, 128))
    m, n = iota((256, 1024), 0), iota((256, 1024), 1)
    same = ((m & 7) == (n >> 7)) & ((m >> 3) == ((n & 127) >> 2))
    gather_ref[...] = jnp.where(same, 1.0, 0.0).astype(bf16)
    twice = jnp.where((iota((K, 128), 1) >> 1) == iota((K, 128), 0), 1.0, 0.0).astype(bf16)
    freqs = jnp.broadcast_to(freqs_ref[...].astype(f32), (8, K)).astype(bf16)
    freq = jnp.dot(freqs, twice, preferred_element_type=f32)[0:1]
    imag = (iota((NT, 128), 1) & 1) == 1
    itab_ref[...] = (wave(freq, imag, (NT, 128), 0) * (1.0 / math.sqrt(K))).astype(bf16)


def fetch_kernel(green_hbm, out_ref, sems):
    rows = K * HERE * 2 // 4
    copies = []
    for n in range(4):
        at = pl.ds(n * rows, rows)
        copies.append(pltpu.make_async_copy(green_hbm.at[at], out_ref.at[at], sems.at[n]))
        copies[-1].start()
    for copy in copies:
        copy.wait()


def product_kernel(left_ref, green_ref, swapped_ref, out_ref, turned_ref):
    a, b = iota((128, 128), 0), iota((128, 128), 1)
    turn = jnp.where((a ^ 1) == b, jnp.where((a & 1) == 1, 1.0, -1.0), 0.0).astype(bf16)
    lane = iota((16, 128), 1)
    is_first = lane < 2 * HERE - WINDOWS[4]
    is_second = (lane >= 2 * HERE - WINDOWS[4]) & (lane < WINDOWS[2] - WINDOWS[4])
    zero = jnp.zeros((16, 128), bf16)

    @pl.loop(0, PAR // 8)
    def _(m):
        for u in range(8):
            x = jnp.dot(left_ref[8 * m + u], turn, preferred_element_type=f32)
            turned_ref[8 * m + u] = x.astype(bf16)

    def pair(i, base):
        total = []
        for half, green_of in enumerate((green_ref, swapped_ref)):

            def part(n, ref):
                return ref[i, n * 32 + half * 16 : n * 32 + half * 16 + 16, :]

            def both(n, ref):
                return jnp.concatenate([part(n, ref), part(n + 1, ref)], axis=1)

            def green(start, count):
                return green_of[pl.ds(base + start, count), :]

            first = jnp.concatenate([both(0, left_ref), both(0, turned_ref)], axis=0)
            second = jnp.concatenate([both(2, left_ref), both(2, turned_ref)], axis=0)
            s, st = part(4, left_ref), part(4, turned_ref)
            shared = [jnp.where(is_first, v, zero) for v in (s, st)]
            shared += [jnp.where(is_second, v, zero) for v in (s, st)]
            shared = jnp.concatenate(shared, axis=0)
            edge = jnp.dot(shared, green(WINDOWS[4], 128), preferred_element_type=f32)
            one = jnp.dot(first, green(WINDOWS[0], 256), preferred_element_type=f32)
            two = jnp.dot(second, green(WINDOWS[2], 256), preferred_element_type=f32)
            total.append((one + edge[0:32], two + edge[32:64]))
        one, two = (p + q for p, q in zip(*total))
        x = (one[0:16], one[16:32], two[0:16], two[16:32])
        for yh in range(2):
            v = jnp.concatenate([g[8 * yh : 8 * yh + 8] for g in x], axis=0)
            out_ref[yh, i] = v.astype(bf16)

    @pl.loop(0, PAR // 8)
    def _(m):
        for u in range(8):
            pair(8 * m + u, pl.multiple_of(m * 4800, 16) + 600 * u)


def smooth_kernel(moved_ref, coef_ref, gather_ref, out_ref, both, grid, sol):
    series = chebyshev_series()

    def start(b, _):
        v = moved_ref[b].astype(f32) + moved_ref[PAR + b].astype(f32)
        v = v.astype(bf16).astype(f32).reshape(4, 8, 128)
        grid[b] = v
        both[0, b + 1] = series[5] * v
        return 0

    lax.fori_loop(0, PAR, start, 0, unroll=4)

    def halo(slot):
        both[slot, 0] = pltpu.roll(both[slot, PAR], 1, 2)
        both[slot, PAR + 1] = pltpu.roll(both[slot, 1], 127, 2)

    for k in range(4, -1, -1):
        now, later = k % 2, (k + 1) % 2
        halo(now)

        def step(b, _, k=k, now=now, later=later):
            def coef(n):
                return coef_ref[n, b]

            u = both[now, b + 1]
            v = coef(0) * u
            v = v + coef(1) * pltpu.roll(u, 4, 2)
            v = v + coef(2) * pltpu.roll(u, 124, 2)
            v = v + coef(3) * both[now, b]
            v = v + coef(4) * both[now, b + 2]
            if k == 0:
                v = 0.5 * v
            v = v + series[k] * grid[b]
            if k < 4:
                v = v - both[later, b + 1]
            if k == 0:
                sol[pl.ds(pl.multiple_of(b * 32, 32), 32), :] = v.reshape(32, 128)
            else:
                both[later, b + 1] = v
            return 0

        lax.fori_loop(0, PAR, step, 0, unroll=UNROLL)
    quarter = iota((32, 128), 1) & 3
    for pair in (0, 16):
        turned = []
        for f in range(8):
            column = []
            for g in (pair, pair + 8):
                x = sol[pl.ds(g + f, 32, stride=32), :]
                column += [jnp.where(quarter == q, x, 0.0).astype(bf16) for q in range(4)]
            turned.append(jnp.concatenate(column, axis=0))
        turned = jnp.concatenate(turned, axis=1)
        y = lax.dot_general(gather_ref[...], turned, NT_DIMS, preferred_element_type=f32)
        for n, g in enumerate((pair, pair + 8)):
            v = y[:, n * 128 : (n + 1) * 128].reshape(ROWS, 8, 128)
            out_ref[:, g : g + 8, :] = v.astype(bf16)


def inverse_kernel(back_ref, itab_ref, out_hbm, wide, mixed, ready, sems):
    wide[...] = back_ref[...].reshape(PAR * 32, 128).astype(f32)
    xs = [wide[pl.ds(r, 128, stride=8), :].astype(bf16) for r in range(8)]
    copies = []
    for n, (start, count) in enumerate(((0, 144), (144, 144), (288, 132))):
        at = pl.ds(start, count)
        itab = itab_ref[at, :]
        for r in range(8):
            y = jnp.dot(itab, xs[r], preferred_element_type=f32)
            mixed[pl.ds(8 * start + r, count, stride=8), :] = y
        y = mixed[8 * start : 8 * (start + count), :].astype(bf16)
        ready[at] = y.reshape(count, 8, 128)
        copies.append(pltpu.make_async_copy(ready.at[at], out_hbm.at[at], sems.at[n]))
        copies[-1].start()
    for copy in copies:
        copy.wait()


def call(kernel, out, in_specs, scratch=(), mib=8, to=VMEM):
    many = isinstance(out, (tuple, list))
    return pl.pallas_call(
        kernel,
        out_shape=out,
        in_specs=in_specs,
        out_specs=[to] * len(out) if many else to,
        scratch_shapes=list(scratch),
        compiler_params=pltpu.CompilerParams(vmem_limit_bytes=mib << 20),
    )


def shape(*dims, dtype=bf16):
    return jax.ShapeDtypeStruct(dims, dtype)


def in_hbm(x):
    return pltpu.with_memory_space_constraint(x, pltpu.HBM)


def partner(bit):
    return [(s * PAR + b, (s ^ bit) * PAR + b) for s in range(SENS) for b in range(PAR)]


def local(data, green, freqs, sensor_order, kappa, theta):
    spectra = call(
        spectra_kernel,
        shape(PAD, 128),
        [HBM, HBM],
        [
            pltpu.VMEM((HERE, R, NT), bf16),
            pltpu.SMEM((K,), i32),
            pltpu.SemaphoreType.DMA((PIECES + 1,)),
        ],
        mib=52,
    )(in_hbm(freqs), in_hbm(jnp.transpose(data, (1, 0, 2))))
    table = green.reshape(K * HERE * 2, 128)
    order = sensor_order.reshape(1, HERE)
    far = lax.ppermute(spectra, AXES, partner(2))
    near = lax.ppermute(spectra, AXES, partner(1))
    fetch = [pltpu.SemaphoreType.DMA((4,))]
    here = call(fetch_kernel, shape(K * HERE * 2, 128), [HBM], fetch)(in_hbm(table))
    order_two = lax.ppermute(order, AXES, partner(1))
    far, near, here, order_two = lax.optimization_barrier((far, near, here, order_two))
    last = lax.ppermute(far, AXES, partner(1))
    last, here = lax.optimization_barrier((last, here))
    swapped = lax.ppermute(here, AXES, partner(1))
    sent = call(slots_kernel, shape(PAR, BLOCK, 128), [VMEM] * 8)(
        spectra, near, far, last, order, order_two, kappa, theta
    )
    left = lax.all_to_all(sent, "par", 0, 0, tiled=True)
    coef, itab, gather = call(
        prior_kernel,
        [shape(5, 32, 8, 128, dtype=f32), shape(NT, 128), shape(256, 1024)],
        [VMEM, VMEM],
    )(freqs.reshape(1, K), left)
    summed = call(
        product_kernel,
        shape(2, PAR, 32, 128),
        [VMEM] * 3,
        [pltpu.VMEM((PAR, BLOCK, 128), bf16)],
    )(left, here, swapped).reshape(2 * PAR, 32, 128)
    groups = [[(2 * y + c) * PAR + b for y in range(2) for b in range(PAR)] for c in range(2)]
    moved = lax.all_to_all(summed, AXES, 0, 0, tiled=True, axis_index_groups=groups)
    smooth = call(
        smooth_kernel,
        shape(ROWS, 32, 128),
        [VMEM] * 3,
        [
            pltpu.VMEM((2, PAR + 2, 4, 8, 128), f32),
            pltpu.VMEM((PAR, 4, 8, 128), f32),
            pltpu.VMEM((PAR * 32, 128), f32),
        ],
    )(moved, coef, gather)
    back = lax.all_to_all(smooth, "par", 0, 0, tiled=True)
    out = call(
        inverse_kernel,
        shape(NT, 8, 128),
        [VMEM, VMEM],
        [
            pltpu.VMEM((PAR * 32, 128), f32),
            pltpu.VMEM((NT * 8, 128), f32),
            pltpu.VMEM((NT, 8, 128), bf16),
            pltpu.SemaphoreType.DMA((3,)),
        ],
        to=HBM,
    )(back, itab)
    return jnp.transpose(out, (1, 0, 2)).reshape(8, NT, 1, 128)


def solution(mesh):
    placed = (
        P(None, "sens", None),
        P(None, "sens", None, "par"),
        P(),
        P("sens"),
        P("par", None),
        P("par", None),
    )
    return jax.shard_map(
        local, mesh=mesh, in_specs=placed, out_specs=P("sens", None, "par", None), check_vma=False
    )
```

```python
import math

import jax
import jax.numpy as jnp
from jax import lax
from jax.experimental import pallas as pl
from jax.experimental.pallas import tpu as pltpu
from jax.sharding import PartitionSpec as P

NT = 420
K = 64
R = 32
ROWS = 32
SWEEPS = 6
SENS = 4
PAR = 32
HERE = 150
PAD = 152
WINDOWS = (0, 128, 344, 472, 256)
BLOCK = 32 * len(WINDOWS)
CHUNK = 80
UNROLL = 16
PIECES = -(-HERE // CHUNK)
AXES = ("sens", "par")
LOWER, UPPER = 0.05, 16.5
f32, bf16, i32 = jnp.float32, jnp.bfloat16, jnp.int32
VMEM = pl.BlockSpec(memory_space=pltpu.VMEM)
SMEM = pl.BlockSpec(memory_space=pltpu.SMEM)
HBM = pl.BlockSpec(memory_space=pltpu.HBM)
NT_DIMS = (((1,), (1,)), ((), ()))
TN_DIMS = (((0,), (0,)), ((), ()))


def iota(shape, dim):
    return lax.broadcasted_iota(i32, shape, dim)


def chebyshev_series():
    d, c = 0.5 * (UPPER + LOWER), 0.5 * (UPPER - LOWER)
    values = []
    for m in range(SWEEPS):
        lam = d - c * math.cos(math.pi * (m + 0.5) / SWEEPS)
        x, res, dirn, alpha = 0.0, 1.0, 0.0, 1.0 / d
        for i in range(SWEEPS):
            beta = 0.0
            if i > 0:
                beta = 0.5 * (c * alpha) ** 2 if i == 1 else (c * alpha / 2.0) ** 2
                alpha = 1.0 / (d - beta / alpha)
            dirn = res + beta * dirn
            x = x + alpha * dirn
            res = res - alpha * lam * dirn
        values.append(x)
    series = [
        2.0 / SWEEPS * sum(v * math.cos(k * math.pi * (m + 0.5) / SWEEPS) for m, v in enumerate(values))
        for k in range(SWEEPS)
    ]
    return [0.5 * series[0]] + series[1:]


def wave(freq, imag, shape, dim):
    t = iota(shape, dim).astype(f32)
    p = t * freq
    m = p - NT * jnp.floor(p * (1.0 / NT))
    m = jnp.where(m < 0, m + NT, m)
    m = jnp.where(m >= NT, m - NT, m)
    m = jnp.where(imag, m + NT // 4, m)
    m = jnp.where(m >= NT, m - NT, m)
    x = (NT // 4 - jnp.minimum(m, NT - m)) * (2.0 * math.pi / NT)
    x2 = x * x
    acc = -1.0 / math.factorial(11) + x2 * (1.0 / math.factorial(13))
    for n, sign in ((9, 1), (7, -1), (5, 1), (3, -1)):
        acc = sign / math.factorial(n) + x2 * acc
    return x + x * x2 * acc


def spectra_kernel(freqs_hbm, data_ref, out_ref, buf, freqs_ref, sems):
    freqs_copy = pltpu.make_async_copy(freqs_hbm, freqs_ref, sems.at[PIECES])
    freqs_copy.start()
    copies = []
    for n in range(PIECES):
        at = pl.ds(n * CHUNK, min(CHUNK, HERE - n * CHUNK))
        copies.append(pltpu.make_async_copy(data_ref.at[at], buf.at[at], sems.at[n]))
        copies[-1].start()
    freqs_copy.wait()
    first = 2 * lax.axis_index("par")
    line = iota((8, NT), 0)
    freq = jnp.where(line < 2, freqs_ref[first], freqs_ref[first + 1]).astype(f32)
    table = wave(freq, (line & 1) == 1, (8, NT), 1) * (1.0 / math.sqrt(NT))
    table = [jnp.broadcast_to(table[j : j + 1], (R, NT)) for j in range(4)]
    table = jnp.concatenate(table, axis=0).astype(bf16)
    own = (iota((R, 128), 1) & 31) == iota((R, 128), 0)
    own = jnp.where(own, 1.0, 0.0).astype(f32).reshape(1, 4, 8, 128)
    fold = (iota((CHUNK, CHUNK * 8), 1) >> 3) == iota((CHUNK, CHUNK * 8), 0)
    fold = jnp.where(fold, 1.0, 0.0).astype(bf16)
    for n, copy in enumerate(copies):
        copy.wait()
        count = min(CHUNK, HERE - n * CHUNK)
        parts = []
        for start in range(0, count, count // 2):
            at = n * CHUNK + start
            x = buf[at : at + count // 2].reshape(count // 2 * R, NT)
            y = lax.dot_general(x, table, NT_DIMS, preferred_element_type=f32)
            y = jnp.sum(y.reshape(count // 2, 4, 8, 128) * own, axis=1)
            parts.append(y.reshape(count // 2 * 8, 128))
        y = jnp.concatenate(parts, axis=0).astype(bf16)
        rows = -(-count // 8) * 8
        y = jnp.dot(fold[:rows, : count * 8], y, preferred_element_type=f32)
        out_ref[n * CHUNK : n * CHUNK + rows, :] = y.astype(bf16)


def split3(x):
    hi = x.astype(bf16).astype(f32)
    mid = (x - hi).astype(bf16).astype(f32)
    return hi, mid, x - hi - mid


def slots_kernel(
    own_ref, core_ref, far_ref, last_ref, order_ref, other_ref, kappa_ref, theta_ref, out_ref
):
    sens = lax.axis_index("sens")
    every = [ref[...] for ref in (own_ref, core_ref, far_ref, last_ref)]
    every = jnp.concatenate(every, axis=0)
    width = 128 * len(WINDOWS)
    at = iota((HERE, width), 1)
    green_row = at
    for n, start in enumerate(WINDOWS):
        green_row = jnp.where((at >> 7) == n, start + (at & 127), green_row)
    slot = jnp.where(green_row >= 2 * HERE, green_row - 2 * HERE, green_row) >> 1
    shared_end = (at >= 4 * 128) & ((at & 127) >= WINDOWS[2] - WINDOWS[4])
    slot = jnp.where(shared_end, -1, slot)
    spread = jnp.where(slot == iota((HERE, width), 0), 1.0, 0.0).astype(bf16)
    lane = iota((R, 128), 1)
    odd = (lane & 1) == 1

    def windows(order):
        block = jnp.where(order >= 150, 1, 0)
        block = jnp.where(order >= 300, 2, block)
        block = jnp.where(order >= 450, 3, block)
        row = (block ^ sens) * PAD + order - HERE * block
        pick = jnp.where(iota((SENS * PAD, HERE), 0) == row, 1.0, 0.0).astype(bf16)
        chosen = lax.dot_general(every, pick, TN_DIMS, preferred_element_type=f32)
        wide = jnp.dot(chosen.astype(bf16), spread, preferred_element_type=f32)
        for n in range(len(WINDOWS)):
            w = wide[:, n * 128 : (n + 1) * 128]
            first = jnp.where(odd, w[32:64], w[0:32])
            second = jnp.where(odd, w[96:128], w[64:96])
            if n < 2:
                v = first
            elif n < 4:
                v = second
            else:
                v = jnp.where(lane < 2 * HERE - WINDOWS[4], first, second)
            zero = (sens & 1) == 0
            yield [jnp.where(zero, v[y : y + 8], v[y + 8 : y + 16]) for y in (0, 16)]

    parts = jnp.zeros((8, 128), f32)
    for n, v in enumerate(split3(kappa_ref[...]) + split3(theta_ref[...])):
        parts = jnp.where(iota((8, 128), 0) == n, v, parts)
    turns = [parts if q == 3 else pltpu.roll(parts, 96 - 32 * q, 1) for q in range(4)]
    rows = []
    for one, two in zip(windows(order_ref[...]), windows(other_ref[...])):
        rows += one + two
    low = iota((8, 128), 1) < 96
    for q in range(4):
        rows[16 + q] = jnp.where(low, rows[16 + q], turns[q])
    block_out = jnp.concatenate(rows, axis=0).astype(bf16)
    for n in range(PAR):
        out_ref[n] = block_out


def prior_kernel(freqs_ref, left_ref, coef_ref, itab_ref, gather_ref):
    flat = left_ref[:, BLOCK - 32 :, :].reshape(PAR * 32, 128)
    lane = iota((32, 128), 1)
    cell = iota((32, 128), 0)
    pick = jnp.where(lane == 96 + cell, 1.0, 0.0).astype(bf16)
    turned = lax.dot_general(pick, flat, NT_DIMS, preferred_element_type=f32).astype(bf16)
    row, to = iota((PAR * 32, 128), 0), iota((PAR * 32, 128), 1)
    here = to == 4 * (row >> 5) + ((row >> 3) & 3)
    part = row & 7
    put = jnp.where(here & (part < 3), 1.0, 0.0).astype(bf16)
    kappa = jnp.dot(turned, put, preferred_element_type=f32)
    put = jnp.where(here & (part >= 3) & (part < 6), 1.0, 0.0).astype(bf16)
    theta = jnp.dot(turned, put, preferred_element_type=f32)
    up, down = lane < 4, lane >= 124
    left = (cell == 0) & ((lane & 3) == 0)
    right = (cell == 31) & ((lane & 3) == 3)
    north = jnp.where(up, theta, pltpu.roll(theta, 4, 1))
    south = jnp.where(down, theta, pltpu.roll(theta, 124, 1))
    back = pltpu.roll(theta, 1, 0)
    west = jnp.where(cell == 0, pltpu.roll(back, 1, 1), back)
    west = jnp.where(left, theta, west)
    ahead = pltpu.roll(theta, 31, 0)
    east = jnp.where(cell == 31, pltpu.roll(ahead, 127, 1), ahead)
    east = jnp.where(right, theta, east)
    north, south, west, east = (0.5 * (theta + v) for v in (north, south, west, east))
    d, c = 0.5 * (UPPER + LOWER), 0.5 * (UPPER - LOWER)
    coefs = [
        (2.0 / c) * (d - (kappa + north + south + west + east)),
        jnp.where(up, 0.0, (2.0 / c) * north),
        jnp.where(down, 0.0, (2.0 / c) * south),
        jnp.where(left, 0.0, (2.0 / c) * west),
        jnp.where(right, 0.0, (2.0 / c) * east),
    ]
    for n, v in enumerate(coefs):
        coef_ref[n] = jnp.broadcast_to(v.reshape(32, 1, 128), (32, 8, 128))
    m, n = iota((256, 1024), 0), iota((256, 1024), 1)
    same = ((m & 7) == (n >> 7)) & ((m >> 3) == ((n & 127) >> 2))
    gather_ref[...] = jnp.where(same, 1.0, 0.0).astype(bf16)
    twice = jnp.where((iota((K, 128), 1) >> 1) == iota((K, 128), 0), 1.0, 0.0).astype(bf16)
    freqs = jnp.broadcast_to(freqs_ref[...].astype(f32), (8, K)).astype(bf16)
    freq = jnp.dot(freqs, twice, preferred_element_type=f32)[0:1]
    imag = (iota((NT, 128), 1) & 1) == 1
    itab_ref[...] = (wave(freq, imag, (NT, 128), 0) * (1.0 / math.sqrt(K))).astype(bf16)


def fetch_kernel(green_hbm, out_ref, sems):
    rows = K * HERE * 2 // 4
    copies = []
    for n in range(4):
        at = pl.ds(n * rows, rows)
        copies.append(pltpu.make_async_copy(green_hbm.at[at], out_ref.at[at], sems.at[n]))
        copies[-1].start()
    for copy in copies:
        copy.wait()


def product_kernel(left_ref, green_ref, swapped_ref, out_hbm, turned_ref, out_ref, sems):
    a, b = iota((128, 128), 0), iota((128, 128), 1)
    turn = jnp.where((a ^ 1) == b, jnp.where((a & 1) == 1, 1.0, -1.0), 0.0).astype(bf16)
    lane = iota((16, 128), 1)
    is_first = lane < 2 * HERE - WINDOWS[4]
    is_second = (lane >= 2 * HERE - WINDOWS[4]) & (lane < WINDOWS[2] - WINDOWS[4])
    zero = jnp.zeros((16, 128), bf16)

    @pl.loop(0, PAR // 8)
    def _(m):
        x = left_ref[pl.ds(8 * m, 8)].reshape(8 * BLOCK, 128)
        x = jnp.dot(x, turn, preferred_element_type=f32).astype(bf16)
        turned_ref[pl.ds(8 * m, 8)] = x.reshape(8, BLOCK, 128)

    def pair(i, base):
        total = []
        for half, green_of in enumerate((green_ref, swapped_ref)):

            def part(n, ref):
                return ref[i, n * 32 + half * 16 : n * 32 + half * 16 + 16, :]

            def both(n, ref):
                return jnp.concatenate([part(n, ref), part(n + 1, ref)], axis=1)

            def green(start, count):
                return green_of[pl.ds(base + start, count), :]

            first = jnp.concatenate([both(0, left_ref), both(0, turned_ref)], axis=0)
            second = jnp.concatenate([both(2, left_ref), both(2, turned_ref)], axis=0)
            s, st = part(4, left_ref), part(4, turned_ref)
            shared = [jnp.where(is_first, v, zero) for v in (s, st)]
            shared += [jnp.where(is_second, v, zero) for v in (s, st)]
            shared = jnp.concatenate(shared, axis=0)
            edge = jnp.dot(shared, green(WINDOWS[4], 128), preferred_element_type=f32)
            one = jnp.dot(first, green(WINDOWS[0], 256), preferred_element_type=f32)
            two = jnp.dot(second, green(WINDOWS[2], 256), preferred_element_type=f32)
            total.append((one + edge[0:32], two + edge[32:64]))
        one, two = (p + q for p, q in zip(*total))
        x = (one[0:16], one[16:32], two[0:16], two[16:32])
        for yh in range(2):
            v = jnp.concatenate([g[8 * yh : 8 * yh + 8] for g in x], axis=0)
            out_ref[yh, i] = v.astype(bf16)

    def piece(m, yh):
        at = pl.ds(8 * m, 8)
        return pltpu.make_async_copy(out_ref.at[yh, at], out_hbm.at[yh, at], sems.at[m, yh])

    @pl.loop(0, PAR // 8)
    def _(m):
        for u in range(8):
            pair(8 * m + u, pl.multiple_of(m * 4800, 16) + 600 * u)
        for yh in range(2):
            piece(m, yh).start()

    for m in range(PAR // 8):
        for yh in range(2):
            piece(m, yh).wait()


def smooth_kernel(moved_ref, coef_ref, gather_ref, out_ref, both, grid, sol):
    series = chebyshev_series()

    def start(b, _):
        v = moved_ref[b].astype(f32) + moved_ref[PAR + b].astype(f32)
        v = v.astype(bf16).astype(f32).reshape(4, 8, 128)
        grid[b] = v
        both[0, b + 1] = series[5] * v
        return 0

    lax.fori_loop(0, PAR, start, 0, unroll=4)

    def halo(slot):
        both[slot, 0] = pltpu.roll(both[slot, PAR], 1, 2)
        both[slot, PAR + 1] = pltpu.roll(both[slot, 1], 127, 2)

    for k in range(4, -1, -1):
        now, later = k % 2, (k + 1) % 2
        halo(now)

        def step(b, _, k=k, now=now, later=later):
            def coef(n):
                return coef_ref[n, b]

            u = both[now, b + 1]
            v = coef(0) * u
            v = v + coef(1) * pltpu.roll(u, 4, 2)
            v = v + coef(2) * pltpu.roll(u, 124, 2)
            v = v + coef(3) * both[now, b]
            v = v + coef(4) * both[now, b + 2]
            if k == 0:
                v = 0.5 * v
            v = v + series[k] * grid[b]
            if k < 4:
                v = v - both[later, b + 1]
            if k == 0:
                sol[pl.ds(pl.multiple_of(b * 32, 32), 32), :] = v.reshape(32, 128)
            else:
                both[later, b + 1] = v
            return 0

        lax.fori_loop(0, PAR, step, 0, unroll=UNROLL)
    quarter = iota((32, 128), 1) & 3
    for pair in (0, 16):
        turned = []
        for f in range(8):
            column = []
            for g in (pair, pair + 8):
                x = sol[pl.ds(g + f, 32, stride=32), :]
                column += [jnp.where(quarter == q, x, 0.0).astype(bf16) for q in range(4)]
            turned.append(jnp.concatenate(column, axis=0))
        turned = jnp.concatenate(turned, axis=1)
        y = lax.dot_general(gather_ref[...], turned, NT_DIMS, preferred_element_type=f32)
        for n, g in enumerate((pair, pair + 8)):
            v = y[:, n * 128 : (n + 1) * 128].reshape(ROWS, 8, 128)
            out_ref[:, g : g + 8, :] = v.astype(bf16)


def inverse_kernel(back_ref, itab_ref, out_hbm, wide, mixed, ready, sems):
    wide[...] = back_ref[...].reshape(PAR * 32, 128).astype(f32)
    xs = [wide[pl.ds(r, 128, stride=8), :].astype(bf16) for r in range(8)]
    copies = []
    for n, (start, count) in enumerate(((0, 144), (144, 144), (288, 132))):
        at = pl.ds(start, count)
        itab = itab_ref[at, :]
        for r in range(8):
            y = jnp.dot(itab, xs[r], preferred_element_type=f32)
            mixed[pl.ds(8 * start + r, count, stride=8), :] = y
        y = mixed[8 * start : 8 * (start + count), :].astype(bf16)
        ready[at] = y.reshape(count, 8, 128)
        copies.append(pltpu.make_async_copy(ready.at[at], out_hbm.at[at], sems.at[n]))
        copies[-1].start()
    for copy in copies:
        copy.wait()


def call(kernel, out, in_specs, scratch=(), mib=8, to=VMEM):
    many = isinstance(out, (tuple, list))
    return pl.pallas_call(
        kernel,
        out_shape=out,
        in_specs=in_specs,
        out_specs=[to] * len(out) if many else to,
        scratch_shapes=list(scratch),
        compiler_params=pltpu.CompilerParams(vmem_limit_bytes=mib << 20),
    )


def shape(*dims, dtype=bf16):
    return jax.ShapeDtypeStruct(dims, dtype)


def in_hbm(x):
    return pltpu.with_memory_space_constraint(x, pltpu.HBM)


def partner(bit):
    return [(s * PAR + b, (s ^ bit) * PAR + b) for s in range(SENS) for b in range(PAR)]


def local(data, green, freqs, sensor_order, kappa, theta):
    spectra = call(
        spectra_kernel,
        shape(PAD, 128),
        [HBM, HBM],
        [
            pltpu.VMEM((HERE, R, NT), bf16),
            pltpu.SMEM((K,), i32),
            pltpu.SemaphoreType.DMA((PIECES + 1,)),
        ],
        mib=52,
    )(in_hbm(freqs), in_hbm(jnp.transpose(data, (1, 0, 2))))
    table = green.reshape(K * HERE * 2, 128)
    order = sensor_order.reshape(1, HERE)
    far = lax.ppermute(spectra, AXES, partner(2))
    near = lax.ppermute(spectra, AXES, partner(1))
    fetch = [pltpu.SemaphoreType.DMA((4,))]
    here = call(fetch_kernel, shape(K * HERE * 2, 128), [HBM], fetch)(in_hbm(table))
    far, near, here, order = lax.optimization_barrier((far, near, here, order))
    order_two = lax.ppermute(order, AXES, partner(1))
    last = lax.ppermute(far, AXES, partner(1))
    last, here = lax.optimization_barrier((last, here))
    swapped = lax.ppermute(here, AXES, partner(1))
    sent = call(slots_kernel, shape(PAR, BLOCK, 128), [VMEM] * 8)(
        spectra, near, far, last, order, order_two, kappa, theta
    )
    left = lax.all_to_all(sent, "par", 0, 0, tiled=True)
    coef, itab, gather = call(
        prior_kernel,
        [shape(5, 32, 8, 128, dtype=f32), shape(NT, 128), shape(256, 1024)],
        [VMEM, VMEM],
    )(freqs.reshape(1, K), left)
    summed = call(
        product_kernel,
        shape(2, PAR, 32, 128),
        [VMEM] * 3,
        [
            pltpu.VMEM((PAR, BLOCK, 128), bf16),
            pltpu.VMEM((2, PAR, 32, 128), bf16),
            pltpu.SemaphoreType.DMA((PAR // 8, 2)),
        ],
        to=HBM,
    )(left, here, swapped).reshape(2 * PAR, 32, 128)
    groups = [[(2 * y + c) * PAR + b for y in range(2) for b in range(PAR)] for c in range(2)]
    moved = lax.all_to_all(summed, AXES, 0, 0, tiled=True, axis_index_groups=groups)
    smooth = call(
        smooth_kernel,
        shape(ROWS, 32, 128),
        [VMEM] * 3,
        [
            pltpu.VMEM((2, PAR + 2, 4, 8, 128), f32),
            pltpu.VMEM((PAR, 4, 8, 128), f32),
            pltpu.VMEM((PAR * 32, 128), f32),
        ],
    )(moved, coef, gather)
    back = lax.all_to_all(smooth, "par", 0, 0, tiled=True)
    out = call(
        inverse_kernel,
        shape(NT, 8, 128),
        [VMEM, VMEM],
        [
            pltpu.VMEM((PAR * 32, 128), f32),
            pltpu.VMEM((NT * 8, 128), f32),
            pltpu.VMEM((NT, 8, 128), bf16),
            pltpu.SemaphoreType.DMA((3,)),
        ],
        to=HBM,
    )(back, itab)
    return jnp.transpose(out, (1, 0, 2)).reshape(8, NT, 1, 128)


def solution(mesh):
    placed = (
        P(None, "sens", None),
        P(None, "sens", None, "par"),
        P(),
        P("sens"),
        P("par", None),
        P("par", None),
    )
    return jax.shard_map(
        local, mesh=mesh, in_specs=placed, out_specs=P("sens", None, "par", None), check_vma=False
    )
```

```python
import math

import jax
import jax.numpy as jnp
from jax import lax
from jax.experimental import pallas as pl
from jax.experimental.pallas import tpu as pltpu
from jax.sharding import PartitionSpec as P

NT = 420
K = 64
R = 32
ROWS = 32
SWEEPS = 6
SENS = 4
PAR = 32
HERE = 150
PAD = 152
WINDOWS = (0, 128, 344, 472, 256)
BLOCK = 32 * len(WINDOWS)
CHUNK = 80
UNROLL = 16
PIECES = -(-HERE // CHUNK)
AXES = ("sens", "par")
LOWER, UPPER = 0.05, 16.5
f32, bf16, i32 = jnp.float32, jnp.bfloat16, jnp.int32
VMEM = pl.BlockSpec(memory_space=pltpu.VMEM)
SMEM = pl.BlockSpec(memory_space=pltpu.SMEM)
HBM = pl.BlockSpec(memory_space=pltpu.HBM)
NT_DIMS = (((1,), (1,)), ((), ()))
TN_DIMS = (((0,), (0,)), ((), ()))


def iota(shape, dim):
    return lax.broadcasted_iota(i32, shape, dim)


def chebyshev_series():
    d, c = 0.5 * (UPPER + LOWER), 0.5 * (UPPER - LOWER)
    values = []
    for m in range(SWEEPS):
        lam = d - c * math.cos(math.pi * (m + 0.5) / SWEEPS)
        x, res, dirn, alpha = 0.0, 1.0, 0.0, 1.0 / d
        for i in range(SWEEPS):
            beta = 0.0
            if i > 0:
                beta = 0.5 * (c * alpha) ** 2 if i == 1 else (c * alpha / 2.0) ** 2
                alpha = 1.0 / (d - beta / alpha)
            dirn = res + beta * dirn
            x = x + alpha * dirn
            res = res - alpha * lam * dirn
        values.append(x)
    series = [
        2.0 / SWEEPS * sum(v * math.cos(k * math.pi * (m + 0.5) / SWEEPS) for m, v in enumerate(values))
        for k in range(SWEEPS)
    ]
    return [0.5 * series[0]] + series[1:]


def wave(freq, imag, shape, dim):
    t = iota(shape, dim).astype(f32)
    p = t * freq
    m = p - NT * jnp.floor(p * (1.0 / NT))
    m = jnp.where(m < 0, m + NT, m)
    m = jnp.where(m >= NT, m - NT, m)
    m = jnp.where(imag, m + NT // 4, m)
    m = jnp.where(m >= NT, m - NT, m)
    x = (NT // 4 - jnp.minimum(m, NT - m)) * (2.0 * math.pi / NT)
    x2 = x * x
    acc = -1.0 / math.factorial(11) + x2 * (1.0 / math.factorial(13))
    for n, sign in ((9, 1), (7, -1), (5, 1), (3, -1)):
        acc = sign / math.factorial(n) + x2 * acc
    return x + x * x2 * acc


def spectra_kernel(freqs_hbm, data_ref, out_ref, buf, freqs_ref, sems):
    freqs_copy = pltpu.make_async_copy(freqs_hbm, freqs_ref, sems.at[PIECES])
    freqs_copy.start()
    copies = []
    for n in range(PIECES):
        at = pl.ds(n * CHUNK, min(CHUNK, HERE - n * CHUNK))
        copies.append(pltpu.make_async_copy(data_ref.at[at], buf.at[at], sems.at[n]))
        copies[-1].start()
    freqs_copy.wait()
    first = 2 * lax.axis_index("par")
    line = iota((8, NT), 0)
    freq = jnp.where(line < 2, freqs_ref[first], freqs_ref[first + 1]).astype(f32)
    table = wave(freq, (line & 1) == 1, (8, NT), 1) * (1.0 / math.sqrt(NT))
    table = [jnp.broadcast_to(table[j : j + 1], (R, NT)) for j in range(4)]
    table = jnp.concatenate(table, axis=0).astype(bf16)
    own = (iota((R, 128), 1) & 31) == iota((R, 128), 0)
    own = jnp.where(own, 1.0, 0.0).astype(f32).reshape(1, 4, 8, 128)
    fold = (iota((CHUNK, CHUNK * 8), 1) >> 3) == iota((CHUNK, CHUNK * 8), 0)
    fold = jnp.where(fold, 1.0, 0.0).astype(bf16)
    for n, copy in enumerate(copies):
        copy.wait()
        count = min(CHUNK, HERE - n * CHUNK)
        parts = []
        for start in range(0, count, count // 2):
            at = n * CHUNK + start
            x = buf[at : at + count // 2].reshape(count // 2 * R, NT)
            y = lax.dot_general(x, table, NT_DIMS, preferred_element_type=f32)
            y = jnp.sum(y.reshape(count // 2, 4, 8, 128) * own, axis=1)
            parts.append(y.reshape(count // 2 * 8, 128))
        y = jnp.concatenate(parts, axis=0).astype(bf16)
        rows = -(-count // 8) * 8
        y = jnp.dot(fold[:rows, : count * 8], y, preferred_element_type=f32)
        out_ref[n * CHUNK : n * CHUNK + rows, :] = y.astype(bf16)


def split3(x):
    hi = x.astype(bf16).astype(f32)
    mid = (x - hi).astype(bf16).astype(f32)
    return hi, mid, x - hi - mid


def slots_kernel(
    own_ref, core_ref, far_ref, last_ref, order_ref, other_ref, kappa_ref, theta_ref, out_ref
):
    sens = lax.axis_index("sens")
    every = [ref[...] for ref in (own_ref, core_ref, far_ref, last_ref)]
    every = jnp.concatenate(every, axis=0)
    width = 128 * len(WINDOWS)
    at = iota((HERE, width), 1)
    green_row = at
    for n, start in enumerate(WINDOWS):
        green_row = jnp.where((at >> 7) == n, start + (at & 127), green_row)
    slot = jnp.where(green_row >= 2 * HERE, green_row - 2 * HERE, green_row) >> 1
    shared_end = (at >= 4 * 128) & ((at & 127) >= WINDOWS[2] - WINDOWS[4])
    slot = jnp.where(shared_end, -1, slot)
    spread = jnp.where(slot == iota((HERE, width), 0), 1.0, 0.0).astype(bf16)
    lane = iota((R, 128), 1)
    odd = (lane & 1) == 1

    def windows(order):
        block = jnp.where(order >= 150, 1, 0)
        block = jnp.where(order >= 300, 2, block)
        block = jnp.where(order >= 450, 3, block)
        row = (block ^ sens) * PAD + order - HERE * block
        pick = jnp.where(iota((SENS * PAD, HERE), 0) == row, 1.0, 0.0).astype(bf16)
        chosen = lax.dot_general(every, pick, TN_DIMS, preferred_element_type=f32)
        wide = jnp.dot(chosen.astype(bf16), spread, preferred_element_type=f32)
        for n in range(len(WINDOWS)):
            w = wide[:, n * 128 : (n + 1) * 128]
            first = jnp.where(odd, w[32:64], w[0:32])
            second = jnp.where(odd, w[96:128], w[64:96])
            if n < 2:
                v = first
            elif n < 4:
                v = second
            else:
                v = jnp.where(lane < 2 * HERE - WINDOWS[4], first, second)
            zero = (sens & 1) == 0
            yield [jnp.where(zero, v[y : y + 8], v[y + 8 : y + 16]) for y in (0, 16)]

    parts = jnp.zeros((8, 128), f32)
    for n, v in enumerate(split3(kappa_ref[...]) + split3(theta_ref[...])):
        parts = jnp.where(iota((8, 128), 0) == n, v, parts)
    turns = [parts if q == 3 else pltpu.roll(parts, 96 - 32 * q, 1) for q in range(4)]
    rows = []
    for one, two in zip(windows(order_ref[...]), windows(other_ref[...])):
        rows += one + two
    low = iota((8, 128), 1) < 96
    for q in range(4):
        rows[16 + q] = jnp.where(low, rows[16 + q], turns[q])
    block_out = jnp.concatenate(rows, axis=0).astype(bf16)
    for n in range(PAR):
        out_ref[n] = block_out


def prior_kernel(freqs_ref, left_ref, coef_ref, itab_ref, gather_ref):
    flat = left_ref[:, BLOCK - 32 :, :].reshape(PAR * 32, 128)
    lane = iota((32, 128), 1)
    cell = iota((32, 128), 0)
    pick = jnp.where(lane == 96 + cell, 1.0, 0.0).astype(bf16)
    turned = lax.dot_general(pick, flat, NT_DIMS, preferred_element_type=f32).astype(bf16)
    row, to = iota((PAR * 32, 128), 0), iota((PAR * 32, 128), 1)
    here = to == 4 * (row >> 5) + ((row >> 3) & 3)
    part = row & 7
    put = jnp.where(here & (part < 3), 1.0, 0.0).astype(bf16)
    kappa = jnp.dot(turned, put, preferred_element_type=f32)
    put = jnp.where(here & (part >= 3) & (part < 6), 1.0, 0.0).astype(bf16)
    theta = jnp.dot(turned, put, preferred_element_type=f32)
    up, down = lane < 4, lane >= 124
    left = (cell == 0) & ((lane & 3) == 0)
    right = (cell == 31) & ((lane & 3) == 3)
    north = jnp.where(up, theta, pltpu.roll(theta, 4, 1))
    south = jnp.where(down, theta, pltpu.roll(theta, 124, 1))
    back = pltpu.roll(theta, 1, 0)
    west = jnp.where(cell == 0, pltpu.roll(back, 1, 1), back)
    west = jnp.where(left, theta, west)
    ahead = pltpu.roll(theta, 31, 0)
    east = jnp.where(cell == 31, pltpu.roll(ahead, 127, 1), ahead)
    east = jnp.where(right, theta, east)
    north, south, west, east = (0.5 * (theta + v) for v in (north, south, west, east))
    d, c = 0.5 * (UPPER + LOWER), 0.5 * (UPPER - LOWER)
    coefs = [
        (2.0 / c) * (d - (kappa + north + south + west + east)),
        jnp.where(up, 0.0, (2.0 / c) * north),
        jnp.where(down, 0.0, (2.0 / c) * south),
        jnp.where(left, 0.0, (2.0 / c) * west),
        jnp.where(right, 0.0, (2.0 / c) * east),
    ]
    for n, v in enumerate(coefs):
        coef_ref[n] = jnp.broadcast_to(v.reshape(32, 1, 128), (32, 8, 128))
    m, n = iota((256, 1024), 0), iota((256, 1024), 1)
    same = ((m & 7) == (n >> 7)) & ((m >> 3) == ((n & 127) >> 2))
    gather_ref[...] = jnp.where(same, 1.0, 0.0).astype(bf16)
    twice = jnp.where((iota((K, 128), 1) >> 1) == iota((K, 128), 0), 1.0, 0.0).astype(bf16)
    freqs = jnp.broadcast_to(freqs_ref[...].astype(f32), (8, K)).astype(bf16)
    freq = jnp.dot(freqs, twice, preferred_element_type=f32)[0:1]
    imag = (iota((NT, 128), 1) & 1) == 1
    itab_ref[...] = (wave(freq, imag, (NT, 128), 0) * (1.0 / math.sqrt(K))).astype(bf16)


def fetch_kernel(green_hbm, out_ref, sems):
    rows = K * HERE * 2 // 4
    copies = []
    for n in range(4):
        at = pl.ds(n * rows, rows)
        copies.append(pltpu.make_async_copy(green_hbm.at[at], out_ref.at[at], sems.at[n]))
        copies[-1].start()
    for copy in copies:
        copy.wait()


def product_kernel(left_ref, green_ref, swapped_ref, out_hbm, turned_ref, out_ref, sems):
    a, b = iota((128, 128), 0), iota((128, 128), 1)
    turn = jnp.where((a ^ 1) == b, jnp.where((a & 1) == 1, 1.0, -1.0), 0.0).astype(bf16)
    lane = iota((16, 128), 1)
    is_first = lane < 2 * HERE - WINDOWS[4]
    is_second = (lane >= 2 * HERE - WINDOWS[4]) & (lane < WINDOWS[2] - WINDOWS[4])
    zero = jnp.zeros((16, 128), bf16)

    @pl.loop(0, PAR // 8)
    def _(m):
        x = left_ref[pl.ds(8 * m, 8)].reshape(8 * BLOCK, 128)
        x = jnp.dot(x, turn, preferred_element_type=f32).astype(bf16)
        turned_ref[pl.ds(8 * m, 8)] = x.reshape(8, BLOCK, 128)

    def pair(i, base):
        total = []
        for half, green_of in enumerate((green_ref, swapped_ref)):

            def part(n, ref):
                return ref[i, n * 32 + half * 16 : n * 32 + half * 16 + 16, :]

            def both(n, ref):
                return jnp.concatenate([part(n, ref), part(n + 1, ref)], axis=1)

            def green(start, count):
                return green_of[pl.ds(base + start, count), :]

            first = jnp.concatenate([both(0, left_ref), both(0, turned_ref)], axis=0)
            second = jnp.concatenate([both(2, left_ref), both(2, turned_ref)], axis=0)
            s, st = part(4, left_ref), part(4, turned_ref)
            shared = [jnp.where(is_first, v, zero) for v in (s, st)]
            shared += [jnp.where(is_second, v, zero) for v in (s, st)]
            shared = jnp.concatenate(shared, axis=0)
            edge = jnp.dot(shared, green(WINDOWS[4], 128), preferred_element_type=f32)
            one = jnp.dot(first, green(WINDOWS[0], 256), preferred_element_type=f32)
            two = jnp.dot(second, green(WINDOWS[2], 256), preferred_element_type=f32)
            total.append((one + edge[0:32], two + edge[32:64]))
        one, two = (p + q for p, q in zip(*total))
        x = (one[0:16], one[16:32], two[0:16], two[16:32])
        for yh in range(2):
            v = jnp.concatenate([g[8 * yh : 8 * yh + 8] for g in x], axis=0)
            out_ref[yh, i] = v.astype(bf16)

    def piece(m, yh):
        at = pl.ds(16 * m, 16)
        return pltpu.make_async_copy(out_ref.at[yh, at], out_hbm.at[yh, at], sems.at[m, yh])

    @pl.loop(0, PAR // 16)
    def _(m):
        for u in range(16):
            pair(16 * m + u, pl.multiple_of(m * 9600, 16) + 600 * u)
        for yh in range(2):
            piece(m, yh).start()

    for m in range(PAR // 16):
        for yh in range(2):
            piece(m, yh).wait()


def smooth_kernel(moved_ref, coef_ref, gather_ref, out_ref, both, grid, sol):
    series = chebyshev_series()

    def start(b, _):
        v = moved_ref[b].astype(f32) + moved_ref[PAR + b].astype(f32)
        v = v.astype(bf16).astype(f32).reshape(4, 8, 128)
        grid[b] = v
        both[0, b + 1] = series[5] * v
        return 0

    lax.fori_loop(0, PAR, start, 0, unroll=UNROLL)

    def halo(slot):
        both[slot, 0] = pltpu.roll(both[slot, PAR], 1, 2)
        both[slot, PAR + 1] = pltpu.roll(both[slot, 1], 127, 2)

    for k in range(4, -1, -1):
        now, later = k % 2, (k + 1) % 2
        halo(now)

        def step(b, _, k=k, now=now, later=later):
            def coef(n):
                return coef_ref[n, b]

            u = both[now, b + 1]
            v = coef(0) * u
            v = v + coef(1) * pltpu.roll(u, 4, 2)
            v = v + coef(2) * pltpu.roll(u, 124, 2)
            v = v + coef(3) * both[now, b]
            v = v + coef(4) * both[now, b + 2]
            if k == 0:
                v = 0.5 * v
            v = v + series[k] * grid[b]
            if k < 4:
                v = v - both[later, b + 1]
            if k == 0:
                sol[pl.ds(pl.multiple_of(b * 32, 32), 32), :] = v.reshape(32, 128)
            else:
                both[later, b + 1] = v
            return 0

        lax.fori_loop(0, PAR, step, 0, unroll=UNROLL)
    quarter = iota((32, 128), 1) & 3
    for pair in (0, 16):
        turned = []
        for f in range(8):
            column = []
            for g in (pair, pair + 8):
                x = sol[pl.ds(g + f, 32, stride=32), :]
                column += [jnp.where(quarter == q, x, 0.0).astype(bf16) for q in range(4)]
            turned.append(jnp.concatenate(column, axis=0))
        turned = jnp.concatenate(turned, axis=1)
        y = lax.dot_general(gather_ref[...], turned, NT_DIMS, preferred_element_type=f32)
        for n, g in enumerate((pair, pair + 8)):
            v = y[:, n * 128 : (n + 1) * 128].reshape(ROWS, 8, 128)
            out_ref[:, g : g + 8, :] = v.astype(bf16)


def inverse_kernel(back_ref, itab_ref, out_hbm, wide, mixed, ready, sems):
    wide[...] = back_ref[...].reshape(PAR * 32, 128).astype(f32)
    xs = [wide[pl.ds(r, 128, stride=8), :].astype(bf16) for r in range(8)]
    copies = []
    for n, (start, count) in enumerate(((0, 144), (144, 144), (288, 132))):
        at = pl.ds(start, count)
        itab = itab_ref[at, :]
        for r in range(8):
            y = jnp.dot(itab, xs[r], preferred_element_type=f32)
            mixed[pl.ds(8 * start + r, count, stride=8), :] = y
        y = mixed[8 * start : 8 * (start + count), :].astype(bf16)
        ready[at] = y.reshape(count, 8, 128)
        copies.append(pltpu.make_async_copy(ready.at[at], out_hbm.at[at], sems.at[n]))
        copies[-1].start()
    for copy in copies:
        copy.wait()


def call(kernel, out, in_specs, scratch=(), mib=8, to=VMEM):
    many = isinstance(out, (tuple, list))
    return pl.pallas_call(
        kernel,
        out_shape=out,
        in_specs=in_specs,
        out_specs=[to] * len(out) if many else to,
        scratch_shapes=list(scratch),
        compiler_params=pltpu.CompilerParams(vmem_limit_bytes=mib << 20),
    )


def shape(*dims, dtype=bf16):
    return jax.ShapeDtypeStruct(dims, dtype)


def in_hbm(x):
    return pltpu.with_memory_space_constraint(x, pltpu.HBM)


def partner(bit):
    return [(s * PAR + b, (s ^ bit) * PAR + b) for s in range(SENS) for b in range(PAR)]


def local(data, green, freqs, sensor_order, kappa, theta):
    spectra = call(
        spectra_kernel,
        shape(PAD, 128),
        [HBM, HBM],
        [
            pltpu.VMEM((HERE, R, NT), bf16),
            pltpu.SMEM((K,), i32),
            pltpu.SemaphoreType.DMA((PIECES + 1,)),
        ],
        mib=52,
    )(in_hbm(freqs), in_hbm(jnp.transpose(data, (1, 0, 2))))
    table = green.reshape(K * HERE * 2, 128)
    order = sensor_order.reshape(1, HERE)
    far = lax.ppermute(spectra, AXES, partner(2))
    near = lax.ppermute(spectra, AXES, partner(1))
    fetch = [pltpu.SemaphoreType.DMA((4,))]
    here = call(fetch_kernel, shape(K * HERE * 2, 128), [HBM], fetch)(in_hbm(table))
    far, near, here, order = lax.optimization_barrier((far, near, here, order))
    order_two = lax.ppermute(order, AXES, partner(1))
    last = lax.ppermute(far, AXES, partner(1))
    last, order_two, here = lax.optimization_barrier((last, order_two, here))
    swapped = lax.ppermute(here, AXES, partner(1))
    sent = call(slots_kernel, shape(PAR, BLOCK, 128), [VMEM] * 8)(
        spectra, near, far, last, order, order_two, kappa, theta
    )
    left = lax.all_to_all(sent, "par", 0, 0, tiled=True)
    coef, itab, gather = call(
        prior_kernel,
        [shape(5, 32, 8, 128, dtype=f32), shape(NT, 128), shape(256, 1024)],
        [VMEM, VMEM],
    )(freqs.reshape(1, K), left)
    summed = call(
        product_kernel,
        shape(2, PAR, 32, 128),
        [VMEM] * 3,
        [
            pltpu.VMEM((PAR, BLOCK, 128), bf16),
            pltpu.VMEM((2, PAR, 32, 128), bf16),
            pltpu.SemaphoreType.DMA((PAR // 16, 2)),
        ],
        to=HBM,
    )(left, here, swapped).reshape(2 * PAR, 32, 128)
    groups = [[(2 * y + c) * PAR + b for y in range(2) for b in range(PAR)] for c in range(2)]
    moved = lax.all_to_all(summed, AXES, 0, 0, tiled=True, axis_index_groups=groups)
    smooth = call(
        smooth_kernel,
        shape(ROWS, 32, 128),
        [VMEM] * 3,
        [
            pltpu.VMEM((2, PAR + 2, 4, 8, 128), f32),
            pltpu.VMEM((PAR, 4, 8, 128), f32),
            pltpu.VMEM((PAR * 32, 128), f32),
        ],
    )(moved, coef, gather)
    back = lax.all_to_all(smooth, "par", 0, 0, tiled=True)
    out = call(
        inverse_kernel,
        shape(NT, 8, 128),
        [VMEM, VMEM],
        [
            pltpu.VMEM((PAR * 32, 128), f32),
            pltpu.VMEM((NT * 8, 128), f32),
            pltpu.VMEM((NT, 8, 128), bf16),
            pltpu.SemaphoreType.DMA((3,)),
        ],
        to=HBM,
    )(back, itab)
    return jnp.transpose(out, (1, 0, 2)).reshape(8, NT, 1, 128)


def solution(mesh):
    placed = (
        P(None, "sens", None),
        P(None, "sens", None, "par"),
        P(),
        P("sens"),
        P("par", None),
        P("par", None),
    )
    return jax.shard_map(
        local, mesh=mesh, in_specs=placed, out_specs=P("sens", None, "par", None), check_vma=False
    )
```

```python
import math

import jax
import jax.numpy as jnp
from jax import lax
from jax.experimental import pallas as pl
from jax.experimental.pallas import tpu as pltpu
from jax.sharding import PartitionSpec as P

NT = 420
K = 64
R = 32
ROWS = 32
SWEEPS = 6
SENS = 4
PAR = 32
HERE = 150
PAD = 152
WINDOWS = (0, 128, 344, 472, 256)
BLOCK = 32 * len(WINDOWS)
CHUNK = 80
UNROLL = 16
PIECES = -(-HERE // CHUNK)
AXES = ("sens", "par")
LOWER, UPPER = 0.05, 16.5
f32, bf16, i32 = jnp.float32, jnp.bfloat16, jnp.int32
VMEM = pl.BlockSpec(memory_space=pltpu.VMEM)
SMEM = pl.BlockSpec(memory_space=pltpu.SMEM)
HBM = pl.BlockSpec(memory_space=pltpu.HBM)
NT_DIMS = (((1,), (1,)), ((), ()))
TN_DIMS = (((0,), (0,)), ((), ()))


def iota(shape, dim):
    return lax.broadcasted_iota(i32, shape, dim)


def chebyshev_series():
    d, c = 0.5 * (UPPER + LOWER), 0.5 * (UPPER - LOWER)
    values = []
    for m in range(SWEEPS):
        lam = d - c * math.cos(math.pi * (m + 0.5) / SWEEPS)
        x, res, dirn, alpha = 0.0, 1.0, 0.0, 1.0 / d
        for i in range(SWEEPS):
            beta = 0.0
            if i > 0:
                beta = 0.5 * (c * alpha) ** 2 if i == 1 else (c * alpha / 2.0) ** 2
                alpha = 1.0 / (d - beta / alpha)
            dirn = res + beta * dirn
            x = x + alpha * dirn
            res = res - alpha * lam * dirn
        values.append(x)
    series = [
        2.0 / SWEEPS * sum(v * math.cos(k * math.pi * (m + 0.5) / SWEEPS) for m, v in enumerate(values))
        for k in range(SWEEPS)
    ]
    return [0.5 * series[0]] + series[1:]


def wave(freq, imag, shape, dim):
    t = iota(shape, dim).astype(f32)
    p = t * freq
    m = p - NT * jnp.floor(p * (1.0 / NT))
    m = jnp.where(m < 0, m + NT, m)
    m = jnp.where(m >= NT, m - NT, m)
    m = jnp.where(imag, m + NT // 4, m)
    m = jnp.where(m >= NT, m - NT, m)
    x = (NT // 4 - jnp.minimum(m, NT - m)) * (2.0 * math.pi / NT)
    x2 = x * x
    acc = -1.0 / math.factorial(11) + x2 * (1.0 / math.factorial(13))
    for n, sign in ((9, 1), (7, -1), (5, 1), (3, -1)):
        acc = sign / math.factorial(n) + x2 * acc
    return x + x * x2 * acc


def spectra_kernel(freqs_hbm, data_ref, out_ref, buf, freqs_ref, sems):
    freqs_copy = pltpu.make_async_copy(freqs_hbm, freqs_ref, sems.at[PIECES])
    freqs_copy.start()
    copies = []
    for n in range(PIECES):
        at = pl.ds(n * CHUNK, min(CHUNK, HERE - n * CHUNK))
        copies.append(pltpu.make_async_copy(data_ref.at[at], buf.at[at], sems.at[n]))
        copies[-1].start()
    freqs_copy.wait()
    first = 2 * lax.axis_index("par")
    line = iota((8, NT), 0)
    freq = jnp.where(line < 2, freqs_ref[first], freqs_ref[first + 1]).astype(f32)
    table = wave(freq, (line & 1) == 1, (8, NT), 1) * (1.0 / math.sqrt(NT))
    table = [jnp.broadcast_to(table[j : j + 1], (R, NT)) for j in range(4)]
    table = jnp.concatenate(table, axis=0).astype(bf16)
    own = (iota((R, 128), 1) & 31) == iota((R, 128), 0)
    own = jnp.where(own, 1.0, 0.0).astype(f32).reshape(1, 4, 8, 128)
    fold = (iota((CHUNK, CHUNK * 8), 1) >> 3) == iota((CHUNK, CHUNK * 8), 0)
    fold = jnp.where(fold, 1.0, 0.0).astype(bf16)
    for n, copy in enumerate(copies):
        copy.wait()
        count = min(CHUNK, HERE - n * CHUNK)
        parts = []
        for start in range(0, count, count // 2):
            at = n * CHUNK + start
            x = buf[at : at + count // 2].reshape(count // 2 * R, NT)
            y = lax.dot_general(x, table, NT_DIMS, preferred_element_type=f32)
            y = jnp.sum(y.reshape(count // 2, 4, 8, 128) * own, axis=1)
            parts.append(y.reshape(count // 2 * 8, 128))
        y = jnp.concatenate(parts, axis=0).astype(bf16)
        rows = -(-count // 8) * 8
        y = jnp.dot(fold[:rows, : count * 8], y, preferred_element_type=f32)
        out_ref[n * CHUNK : n * CHUNK + rows, :] = y.astype(bf16)


def split3(x):
    hi = x.astype(bf16).astype(f32)
    mid = (x - hi).astype(bf16).astype(f32)
    return hi, mid, x - hi - mid


def slots_kernel(
    own_ref, core_ref, far_ref, last_ref, order_ref, other_ref, kappa_ref, theta_ref, out_ref
):
    sens = lax.axis_index("sens")
    every = [ref[...] for ref in (own_ref, core_ref, far_ref, last_ref)]
    every = jnp.concatenate(every, axis=0)
    width = 128 * len(WINDOWS)
    at = iota((HERE, width), 1)
    green_row = at
    for n, start in enumerate(WINDOWS):
        green_row = jnp.where((at >> 7) == n, start + (at & 127), green_row)
    slot = jnp.where(green_row >= 2 * HERE, green_row - 2 * HERE, green_row) >> 1
    shared_end = (at >= 4 * 128) & ((at & 127) >= WINDOWS[2] - WINDOWS[4])
    slot = jnp.where(shared_end, -1, slot)
    spread = jnp.where(slot == iota((HERE, width), 0), 1.0, 0.0).astype(bf16)
    lane = iota((R, 128), 1)
    odd = (lane & 1) == 1

    def windows(order):
        block = jnp.where(order >= 150, 1, 0)
        block = jnp.where(order >= 300, 2, block)
        block = jnp.where(order >= 450, 3, block)
        row = (block ^ sens) * PAD + order - HERE * block
        pick = jnp.where(iota((SENS * PAD, HERE), 0) == row, 1.0, 0.0).astype(bf16)
        chosen = lax.dot_general(every, pick, TN_DIMS, preferred_element_type=f32)
        wide = jnp.dot(chosen.astype(bf16), spread, preferred_element_type=f32)
        for n in range(len(WINDOWS)):
            w = wide[:, n * 128 : (n + 1) * 128]
            first = jnp.where(odd, w[32:64], w[0:32])
            second = jnp.where(odd, w[96:128], w[64:96])
            if n < 2:
                v = first
            elif n < 4:
                v = second
            else:
                v = jnp.where(lane < 2 * HERE - WINDOWS[4], first, second)
            zero = (sens & 1) == 0
            yield [jnp.where(zero, v[y : y + 8], v[y + 8 : y + 16]) for y in (0, 16)]

    parts = jnp.zeros((8, 128), f32)
    for n, v in enumerate(split3(kappa_ref[...]) + split3(theta_ref[...])):
        parts = jnp.where(iota((8, 128), 0) == n, v, parts)
    turns = [parts if q == 3 else pltpu.roll(parts, 96 - 32 * q, 1) for q in range(4)]
    rows = []
    for one, two in zip(windows(order_ref[...]), windows(other_ref[...])):
        rows += one + two
    low = iota((8, 128), 1) < 96
    for q in range(4):
        rows[16 + q] = jnp.where(low, rows[16 + q], turns[q])
    block_out = jnp.concatenate(rows, axis=0).astype(bf16)
    for n in range(PAR):
        out_ref[n] = block_out


def coefficients(left_ref, coef_ref):
    flat = left_ref[:, BLOCK - 32 :, :].reshape(PAR * 32, 128)
    lane = iota((32, 128), 1)
    cell = iota((32, 128), 0)
    pick = jnp.where(lane == 96 + cell, 1.0, 0.0).astype(bf16)
    turned = lax.dot_general(pick, flat, NT_DIMS, preferred_element_type=f32).astype(bf16)
    row, to = iota((PAR * 32, 128), 0), iota((PAR * 32, 128), 1)
    here = to == 4 * (row >> 5) + ((row >> 3) & 3)
    part = row & 7
    put = jnp.where(here & (part < 3), 1.0, 0.0).astype(bf16)
    kappa = jnp.dot(turned, put, preferred_element_type=f32)
    put = jnp.where(here & (part >= 3) & (part < 6), 1.0, 0.0).astype(bf16)
    theta = jnp.dot(turned, put, preferred_element_type=f32)
    up, down = lane < 4, lane >= 124
    left = (cell == 0) & ((lane & 3) == 0)
    right = (cell == 31) & ((lane & 3) == 3)
    north = jnp.where(up, theta, pltpu.roll(theta, 4, 1))
    south = jnp.where(down, theta, pltpu.roll(theta, 124, 1))
    back = pltpu.roll(theta, 1, 0)
    west = jnp.where(cell == 0, pltpu.roll(back, 1, 1), back)
    west = jnp.where(left, theta, west)
    ahead = pltpu.roll(theta, 31, 0)
    east = jnp.where(cell == 31, pltpu.roll(ahead, 127, 1), ahead)
    east = jnp.where(right, theta, east)
    north, south, west, east = (0.5 * (theta + v) for v in (north, south, west, east))
    d, c = 0.5 * (UPPER + LOWER), 0.5 * (UPPER - LOWER)
    coefs = [
        (2.0 / c) * (d - (kappa + north + south + west + east)),
        jnp.where(up, 0.0, (2.0 / c) * north),
        jnp.where(down, 0.0, (2.0 / c) * south),
        jnp.where(left, 0.0, (2.0 / c) * west),
        jnp.where(right, 0.0, (2.0 / c) * east),
    ]
    for n, v in enumerate(coefs):
        coef_ref[n] = jnp.broadcast_to(v.reshape(32, 1, 128), (32, 8, 128))


def tables(freqs_ref, itab_ref, gather_ref):
    m, n = iota((256, 1024), 0), iota((256, 1024), 1)
    same = ((m & 7) == (n >> 7)) & ((m >> 3) == ((n & 127) >> 2))
    gather_ref[...] = jnp.where(same, 1.0, 0.0).astype(bf16)
    twice = jnp.where((iota((K, 128), 1) >> 1) == iota((K, 128), 0), 1.0, 0.0).astype(bf16)
    freqs = jnp.broadcast_to(freqs_ref[...].astype(f32), (8, K)).astype(bf16)
    freq = jnp.dot(freqs, twice, preferred_element_type=f32)[0:1]
    imag = (iota((NT, 128), 1) & 1) == 1
    itab_ref[...] = (wave(freq, imag, (NT, 128), 0) * (1.0 / math.sqrt(K))).astype(bf16)


def fetch_kernel(green_hbm, freqs_ref, out_ref, itab_ref, gather_ref, sems):
    rows = K * HERE * 2 // 4
    copies = []
    for n in range(4):
        at = pl.ds(n * rows, rows)
        copies.append(pltpu.make_async_copy(green_hbm.at[at], out_ref.at[at], sems.at[n]))
        copies[-1].start()
    tables(freqs_ref, itab_ref, gather_ref)
    for copy in copies:
        copy.wait()


def product_kernel(left_ref, green_ref, swapped_ref, out_ref, turned_ref):
    a, b = iota((128, 128), 0), iota((128, 128), 1)
    turn = jnp.where((a ^ 1) == b, jnp.where((a & 1) == 1, 1.0, -1.0), 0.0).astype(bf16)
    lane = iota((16, 128), 1)
    is_first = lane < 2 * HERE - WINDOWS[4]
    is_second = (lane >= 2 * HERE - WINDOWS[4]) & (lane < WINDOWS[2] - WINDOWS[4])
    zero = jnp.zeros((16, 128), bf16)

    @pl.loop(0, PAR // 8)
    def _(m):
        x = left_ref[pl.ds(8 * m, 8)].reshape(8 * BLOCK, 128)
        x = jnp.dot(x, turn, preferred_element_type=f32).astype(bf16)
        turned_ref[pl.ds(8 * m, 8)] = x.reshape(8, BLOCK, 128)

    def pair(i, base):
        total = []
        for half, green_of in enumerate((green_ref, swapped_ref)):

            def part(n, ref):
                return ref[i, n * 32 + half * 16 : n * 32 + half * 16 + 16, :]

            def both(n, ref):
                return jnp.concatenate([part(n, ref), part(n + 1, ref)], axis=1)

            def green(start, count):
                return green_of[pl.ds(base + start, count), :]

            first = jnp.concatenate([both(0, left_ref), both(0, turned_ref)], axis=0)
            second = jnp.concatenate([both(2, left_ref), both(2, turned_ref)], axis=0)
            s, st = part(4, left_ref), part(4, turned_ref)
            shared = [jnp.where(is_first, v, zero) for v in (s, st)]
            shared += [jnp.where(is_second, v, zero) for v in (s, st)]
            shared = jnp.concatenate(shared, axis=0)
            edge = jnp.dot(shared, green(WINDOWS[4], 128), preferred_element_type=f32)
            one = jnp.dot(first, green(WINDOWS[0], 256), preferred_element_type=f32)
            two = jnp.dot(second, green(WINDOWS[2], 256), preferred_element_type=f32)
            total.append((one + edge[0:32], two + edge[32:64]))
        one, two = (p + q for p, q in zip(*total))
        x = (one[0:16], one[16:32], two[0:16], two[16:32])
        for yh in range(2):
            v = jnp.concatenate([g[8 * yh : 8 * yh + 8] for g in x], axis=0)
            out_ref[yh, i] = v.astype(bf16)

    @pl.loop(0, PAR // 16)
    def _(m):
        for u in range(16):
            pair(16 * m + u, pl.multiple_of(m * 9600, 16) + 600 * u)


def smooth_kernel(moved_ref, left_ref, gather_ref, out_ref, both, grid, sol, coef_ref):
    coefficients(left_ref, coef_ref)
    series = chebyshev_series()

    def start(b, _):
        v = moved_ref[b].astype(f32) + moved_ref[PAR + b].astype(f32)
        v = v.astype(bf16).astype(f32).reshape(4, 8, 128)
        grid[b] = v
        both[0, b + 1] = series[5] * v
        return 0

    lax.fori_loop(0, PAR, start, 0, unroll=UNROLL)

    def halo(slot):
        both[slot, 0] = pltpu.roll(both[slot, PAR], 1, 2)
        both[slot, PAR + 1] = pltpu.roll(both[slot, 1], 127, 2)

    for k in range(4, -1, -1):
        now, later = k % 2, (k + 1) % 2
        halo(now)

        def step(b, _, k=k, now=now, later=later):
            def coef(n):
                return coef_ref[n, b]

            u = both[now, b + 1]
            v = coef(0) * u
            v = v + coef(1) * pltpu.roll(u, 4, 2)
            v = v + coef(2) * pltpu.roll(u, 124, 2)
            v = v + coef(3) * both[now, b]
            v = v + coef(4) * both[now, b + 2]
            if k == 0:
                v = 0.5 * v
            v = v + series[k] * grid[b]
            if k < 4:
                v = v - both[later, b + 1]
            if k == 0:
                sol[pl.ds(pl.multiple_of(b * 32, 32), 32), :] = v.reshape(32, 128)
            else:
                both[later, b + 1] = v
            return 0

        lax.fori_loop(0, PAR, step, 0, unroll=UNROLL)
    quarter = iota((32, 128), 1) & 3
    for pair in (0, 16):
        turned = []
        for f in range(8):
            column = []
            for g in (pair, pair + 8):
                x = sol[pl.ds(g + f, 32, stride=32), :]
                column += [jnp.where(quarter == q, x, 0.0).astype(bf16) for q in range(4)]
            turned.append(jnp.concatenate(column, axis=0))
        turned = jnp.concatenate(turned, axis=1)
        y = lax.dot_general(gather_ref[...], turned, NT_DIMS, preferred_element_type=f32)
        for n, g in enumerate((pair, pair + 8)):
            v = y[:, n * 128 : (n + 1) * 128].reshape(ROWS, 8, 128)
            out_ref[:, g : g + 8, :] = v.astype(bf16)


def inverse_kernel(back_ref, itab_ref, out_hbm, wide, mixed, ready, sems):
    wide[...] = back_ref[...].reshape(PAR * 32, 128).astype(f32)
    xs = [wide[pl.ds(r, 128, stride=8), :].astype(bf16) for r in range(8)]
    copies = []
    for n, (start, count) in enumerate(((0, 144), (144, 144), (288, 132))):
        at = pl.ds(start, count)
        itab = itab_ref[at, :]
        for r in range(8):
            y = jnp.dot(itab, xs[r], preferred_element_type=f32)
            mixed[pl.ds(8 * start + r, count, stride=8), :] = y
        y = mixed[8 * start : 8 * (start + count), :].astype(bf16)
        ready[at] = y.reshape(count, 8, 128)
        copies.append(pltpu.make_async_copy(ready.at[at], out_hbm.at[at], sems.at[n]))
        copies[-1].start()
    for copy in copies:
        copy.wait()


def call(kernel, out, in_specs, scratch=(), mib=8, to=VMEM):
    many = isinstance(out, (tuple, list))
    return pl.pallas_call(
        kernel,
        out_shape=out,
        in_specs=in_specs,
        out_specs=[to] * len(out) if many else to,
        scratch_shapes=list(scratch),
        compiler_params=pltpu.CompilerParams(vmem_limit_bytes=mib << 20),
    )


def shape(*dims, dtype=bf16):
    return jax.ShapeDtypeStruct(dims, dtype)


def in_hbm(x):
    return pltpu.with_memory_space_constraint(x, pltpu.HBM)


def partner(bit):
    return [(s * PAR + b, (s ^ bit) * PAR + b) for s in range(SENS) for b in range(PAR)]


def local(data, green, freqs, sensor_order, kappa, theta):
    spectra = call(
        spectra_kernel,
        shape(PAD, 128),
        [HBM, HBM],
        [
            pltpu.VMEM((HERE, R, NT), bf16),
            pltpu.SMEM((K,), i32),
            pltpu.SemaphoreType.DMA((PIECES + 1,)),
        ],
        mib=52,
    )(in_hbm(freqs), in_hbm(jnp.transpose(data, (1, 0, 2))))
    table = green.reshape(K * HERE * 2, 128)
    order = sensor_order.reshape(1, HERE)
    far = lax.ppermute(spectra, AXES, partner(2))
    near = lax.ppermute(spectra, AXES, partner(1))
    here, itab, gather = call(
        fetch_kernel,
        [shape(K * HERE * 2, 128), shape(NT, 128), shape(256, 1024)],
        [HBM, VMEM],
        [pltpu.SemaphoreType.DMA((4,))],
    )(in_hbm(table), freqs.reshape(1, K))
    far, near, here, order = lax.optimization_barrier((far, near, here, order))
    order_two = lax.ppermute(order, AXES, partner(1))
    last = lax.ppermute(far, AXES, partner(1))
    last, order_two, here = lax.optimization_barrier((last, order_two, here))
    swapped = lax.ppermute(here, AXES, partner(1))
    sent = call(slots_kernel, shape(PAR, BLOCK, 128), [VMEM] * 8)(
        spectra, near, far, last, order, order_two, kappa, theta
    )
    left = lax.all_to_all(sent, "par", 0, 0, tiled=True)
    summed = call(
        product_kernel,
        shape(2, PAR, 32, 128),
        [VMEM] * 3,
        [
            pltpu.VMEM((PAR, BLOCK, 128), bf16),
        ],
    )(left, here, swapped).reshape(2 * PAR, 32, 128)
    groups = [[(2 * y + c) * PAR + b for y in range(2) for b in range(PAR)] for c in range(2)]
    moved = lax.all_to_all(summed, AXES, 0, 0, tiled=True, axis_index_groups=groups)
    smooth = call(
        smooth_kernel,
        shape(ROWS, 32, 128),
        [VMEM] * 3,
        [
            pltpu.VMEM((2, PAR + 2, 4, 8, 128), f32),
            pltpu.VMEM((PAR, 4, 8, 128), f32),
            pltpu.VMEM((PAR * 32, 128), f32),
            pltpu.VMEM((5, 32, 8, 128), f32),
        ],
    )(moved, left, gather)
    back = lax.all_to_all(smooth, "par", 0, 0, tiled=True)
    out = call(
        inverse_kernel,
        shape(NT, 8, 128),
        [VMEM, VMEM],
        [
            pltpu.VMEM((PAR * 32, 128), f32),
            pltpu.VMEM((NT * 8, 128), f32),
            pltpu.VMEM((NT, 8, 128), bf16),
            pltpu.SemaphoreType.DMA((3,)),
        ],
        to=HBM,
    )(back, itab)
    return jnp.transpose(out, (1, 0, 2)).reshape(8, NT, 1, 128)


def solution(mesh):
    placed = (
        P(None, "sens", None),
        P(None, "sens", None, "par"),
        P(),
        P("sens"),
        P("par", None),
        P("par", None),
    )
    return jax.shard_map(
        local, mesh=mesh, in_specs=placed, out_specs=P("sens", None, "par", None), check_vma=False
    )
```

```python
import math

import jax
import jax.numpy as jnp
from jax import lax
from jax.experimental import pallas as pl
from jax.experimental.pallas import tpu as pltpu
from jax.sharding import PartitionSpec as P

NT = 420
K = 64
R = 32
ROWS = 32
SWEEPS = 6
SENS = 4
PAR = 32
HERE = 150
PAD = 152
WINDOWS = (0, 128, 344, 472, 256)
BLOCK = 32 * len(WINDOWS)
CHUNK = 80
UNROLL = 16
PIECES = -(-HERE // CHUNK)
AXES = ("sens", "par")
LOWER, UPPER = 0.05, 16.5
f32, bf16, i32 = jnp.float32, jnp.bfloat16, jnp.int32
VMEM = pl.BlockSpec(memory_space=pltpu.VMEM)
SMEM = pl.BlockSpec(memory_space=pltpu.SMEM)
HBM = pl.BlockSpec(memory_space=pltpu.HBM)
NT_DIMS = (((1,), (1,)), ((), ()))
TN_DIMS = (((0,), (0,)), ((), ()))


def iota(shape, dim):
    return lax.broadcasted_iota(i32, shape, dim)


def chebyshev_series():
    d, c = 0.5 * (UPPER + LOWER), 0.5 * (UPPER - LOWER)
    values = []
    for m in range(SWEEPS):
        lam = d - c * math.cos(math.pi * (m + 0.5) / SWEEPS)
        x, res, dirn, alpha = 0.0, 1.0, 0.0, 1.0 / d
        for i in range(SWEEPS):
            beta = 0.0
            if i > 0:
                beta = 0.5 * (c * alpha) ** 2 if i == 1 else (c * alpha / 2.0) ** 2
                alpha = 1.0 / (d - beta / alpha)
            dirn = res + beta * dirn
            x = x + alpha * dirn
            res = res - alpha * lam * dirn
        values.append(x)
    series = [
        2.0 / SWEEPS * sum(v * math.cos(k * math.pi * (m + 0.5) / SWEEPS) for m, v in enumerate(values))
        for k in range(SWEEPS)
    ]
    return [0.5 * series[0]] + series[1:]


def wave(freq, imag, shape, dim):
    t = iota(shape, dim).astype(f32)
    p = t * freq
    m = p - NT * jnp.floor(p * (1.0 / NT))
    m = jnp.where(m < 0, m + NT, m)
    m = jnp.where(m >= NT, m - NT, m)
    m = jnp.where(imag, m + NT // 4, m)
    m = jnp.where(m >= NT, m - NT, m)
    x = (NT // 4 - jnp.minimum(m, NT - m)) * (2.0 * math.pi / NT)
    x2 = x * x
    acc = -1.0 / math.factorial(11) + x2 * (1.0 / math.factorial(13))
    for n, sign in ((9, 1), (7, -1), (5, 1), (3, -1)):
        acc = sign / math.factorial(n) + x2 * acc
    return x + x * x2 * acc


def spectra_kernel(freqs_hbm, data_ref, out_ref, buf, freqs_ref, sems):
    freqs_copy = pltpu.make_async_copy(freqs_hbm, freqs_ref, sems.at[PIECES])
    freqs_copy.start()
    copies = []
    for n in range(PIECES):
        at = pl.ds(n * CHUNK, min(CHUNK, HERE - n * CHUNK))
        copies.append(pltpu.make_async_copy(data_ref.at[at], buf.at[at], sems.at[n]))
        copies[-1].start()
    freqs_copy.wait()
    first = 2 * lax.axis_index("par")
    line = iota((8, NT), 0)
    freq = jnp.where(line < 2, freqs_ref[first], freqs_ref[first + 1]).astype(f32)
    table = wave(freq, (line & 1) == 1, (8, NT), 1) * (1.0 / math.sqrt(NT))
    table = [jnp.broadcast_to(table[j : j + 1], (R, NT)) for j in range(4)]
    table = jnp.concatenate(table, axis=0).astype(bf16)
    own = (iota((R, 128), 1) & 31) == iota((R, 128), 0)
    own = jnp.where(own, 1.0, 0.0).astype(f32).reshape(1, 4, 8, 128)
    fold = (iota((CHUNK, CHUNK * 8), 1) >> 3) == iota((CHUNK, CHUNK * 8), 0)
    fold = jnp.where(fold, 1.0, 0.0).astype(bf16)
    for n, copy in enumerate(copies):
        copy.wait()
        count = min(CHUNK, HERE - n * CHUNK)
        parts = []
        for start in range(0, count, count // 2):
            at = n * CHUNK + start
            x = buf[at : at + count // 2].reshape(count // 2 * R, NT)
            y = lax.dot_general(x, table, NT_DIMS, preferred_element_type=f32)
            y = jnp.sum(y.reshape(count // 2, 4, 8, 128) * own, axis=1)
            parts.append(y.reshape(count // 2 * 8, 128))
        y = jnp.concatenate(parts, axis=0).astype(bf16)
        rows = -(-count // 8) * 8
        y = jnp.dot(fold[:rows, : count * 8], y, preferred_element_type=f32)
        out_ref[n * CHUNK : n * CHUNK + rows, :] = y.astype(bf16)


def split3(x):
    hi = x.astype(bf16).astype(f32)
    mid = (x - hi).astype(bf16).astype(f32)
    return hi, mid, x - hi - mid


def slots_kernel(
    own_ref, core_ref, far_ref, last_ref, order_ref, other_ref, kappa_ref, theta_ref, out_ref
):
    sens = lax.axis_index("sens")
    every = [ref[...] for ref in (own_ref, core_ref, far_ref, last_ref)]
    every = jnp.concatenate(every, axis=0)
    width = 128 * len(WINDOWS)
    at = iota((HERE, width), 1)
    green_row = at
    for n, start in enumerate(WINDOWS):
        green_row = jnp.where((at >> 7) == n, start + (at & 127), green_row)
    slot = jnp.where(green_row >= 2 * HERE, green_row - 2 * HERE, green_row) >> 1
    shared_end = (at >= 4 * 128) & ((at & 127) >= WINDOWS[2] - WINDOWS[4])
    slot = jnp.where(shared_end, -1, slot)
    spread = jnp.where(slot == iota((HERE, width), 0), 1.0, 0.0).astype(bf16)
    lane = iota((R, 128), 1)
    odd = (lane & 1) == 1

    def windows(order):
        block = jnp.where(order >= 150, 1, 0)
        block = jnp.where(order >= 300, 2, block)
        block = jnp.where(order >= 450, 3, block)
        row = (block ^ sens) * PAD + order - HERE * block
        pick = jnp.where(iota((SENS * PAD, HERE), 0) == row, 1.0, 0.0).astype(bf16)
        chosen = lax.dot_general(every, pick, TN_DIMS, preferred_element_type=f32)
        wide = jnp.dot(chosen.astype(bf16), spread, preferred_element_type=f32)
        for n in range(len(WINDOWS)):
            w = wide[:, n * 128 : (n + 1) * 128]
            first = jnp.where(odd, w[32:64], w[0:32])
            second = jnp.where(odd, w[96:128], w[64:96])
            if n < 2:
                v = first
            elif n < 4:
                v = second
            else:
                v = jnp.where(lane < 2 * HERE - WINDOWS[4], first, second)
            zero = (sens & 1) == 0
            yield [jnp.where(zero, v[y : y + 8], v[y + 8 : y + 16]) for y in (0, 16)]

    parts = jnp.zeros((8, 128), f32)
    for n, v in enumerate(split3(kappa_ref[...]) + split3(theta_ref[...])):
        parts = jnp.where(iota((8, 128), 0) == n, v, parts)
    turns = [parts if q == 3 else pltpu.roll(parts, 96 - 32 * q, 1) for q in range(4)]
    rows = []
    for one, two in zip(windows(order_ref[...]), windows(other_ref[...])):
        rows += one + two
    low = iota((8, 128), 1) < 96
    for q in range(4):
        rows[16 + q] = jnp.where(low, rows[16 + q], turns[q])
    block_out = jnp.concatenate(rows, axis=0).astype(bf16)
    for n in range(PAR):
        out_ref[n] = block_out


def coefficients(left_ref, put_ref, coef_ref):
    flat = left_ref[:, BLOCK - 32 :, :].reshape(PAR * 32, 128)
    lane = iota((32, 128), 1)
    cell = iota((32, 128), 0)
    pick = jnp.where(lane == 96 + cell, 1.0, 0.0).astype(bf16)
    turned = lax.dot_general(pick, flat, NT_DIMS, preferred_element_type=f32).astype(bf16)
    kappa = jnp.dot(turned, put_ref[0], preferred_element_type=f32)
    theta = jnp.dot(turned, put_ref[1], preferred_element_type=f32)
    up, down = lane < 4, lane >= 124
    left = (cell == 0) & ((lane & 3) == 0)
    right = (cell == 31) & ((lane & 3) == 3)
    north = jnp.where(up, theta, pltpu.roll(theta, 4, 1))
    south = jnp.where(down, theta, pltpu.roll(theta, 124, 1))
    back = pltpu.roll(theta, 1, 0)
    west = jnp.where(cell == 0, pltpu.roll(back, 1, 1), back)
    west = jnp.where(left, theta, west)
    ahead = pltpu.roll(theta, 31, 0)
    east = jnp.where(cell == 31, pltpu.roll(ahead, 127, 1), ahead)
    east = jnp.where(right, theta, east)
    north, south, west, east = (0.5 * (theta + v) for v in (north, south, west, east))
    d, c = 0.5 * (UPPER + LOWER), 0.5 * (UPPER - LOWER)
    coefs = [
        (2.0 / c) * (d - (kappa + north + south + west + east)),
        jnp.where(up, 0.0, (2.0 / c) * north),
        jnp.where(down, 0.0, (2.0 / c) * south),
        jnp.where(left, 0.0, (2.0 / c) * west),
        jnp.where(right, 0.0, (2.0 / c) * east),
    ]
    for n, v in enumerate(coefs):
        coef_ref[n] = jnp.broadcast_to(v.reshape(32, 1, 128), (32, 8, 128))


def tables(freqs_ref, itab_ref, gather_ref, put_ref):
    row, to = iota((PAR * 32, 128), 0), iota((PAR * 32, 128), 1)
    here = to == 4 * (row >> 5) + ((row >> 3) & 3)
    part = row & 7
    put_ref[0] = jnp.where(here & (part < 3), 1.0, 0.0).astype(bf16)
    put_ref[1] = jnp.where(here & (part >= 3) & (part < 6), 1.0, 0.0).astype(bf16)
    m, n = iota((256, 1024), 0), iota((256, 1024), 1)
    same = ((m & 7) == (n >> 7)) & ((m >> 3) == ((n & 127) >> 2))
    gather_ref[...] = jnp.where(same, 1.0, 0.0).astype(bf16)
    twice = jnp.where((iota((K, 128), 1) >> 1) == iota((K, 128), 0), 1.0, 0.0).astype(bf16)
    freqs = jnp.broadcast_to(freqs_ref[...].astype(f32), (8, K)).astype(bf16)
    freq = jnp.dot(freqs, twice, preferred_element_type=f32)[0:1]
    imag = (iota((NT, 128), 1) & 1) == 1
    itab_ref[...] = (wave(freq, imag, (NT, 128), 0) * (1.0 / math.sqrt(K))).astype(bf16)


def fetch_kernel(green_hbm, freqs_ref, out_ref, itab_ref, gather_ref, put_ref, sems):
    rows = K * HERE * 2 // 4
    copies = []
    for n in range(4):
        at = pl.ds(n * rows, rows)
        copies.append(pltpu.make_async_copy(green_hbm.at[at], out_ref.at[at], sems.at[n]))
        copies[-1].start()
    tables(freqs_ref, itab_ref, gather_ref, put_ref)
    for copy in copies:
        copy.wait()


def product_kernel(left_ref, green_ref, swapped_ref, out_ref, turned_ref):
    a, b = iota((128, 128), 0), iota((128, 128), 1)
    turn = jnp.where((a ^ 1) == b, jnp.where((a & 1) == 1, 1.0, -1.0), 0.0).astype(bf16)
    lane = iota((16, 128), 1)
    is_first = lane < 2 * HERE - WINDOWS[4]
    is_second = (lane >= 2 * HERE - WINDOWS[4]) & (lane < WINDOWS[2] - WINDOWS[4])
    zero = jnp.zeros((16, 128), bf16)

    @pl.loop(0, PAR // 8)
    def _(m):
        x = left_ref[pl.ds(8 * m, 8)].reshape(8 * BLOCK, 128)
        x = jnp.dot(x, turn, preferred_element_type=f32).astype(bf16)
        turned_ref[pl.ds(8 * m, 8)] = x.reshape(8, BLOCK, 128)

    def pair(i, base):
        total = []
        for half, green_of in enumerate((green_ref, swapped_ref)):

            def part(n, ref):
                return ref[i, n * 32 + half * 16 : n * 32 + half * 16 + 16, :]

            def both(n, ref):
                return jnp.concatenate([part(n, ref), part(n + 1, ref)], axis=1)

            def green(start, count):
                return green_of[pl.ds(base + start, count), :]

            first = jnp.concatenate([both(0, left_ref), both(0, turned_ref)], axis=0)
            second = jnp.concatenate([both(2, left_ref), both(2, turned_ref)], axis=0)
            s, st = part(4, left_ref), part(4, turned_ref)
            shared = [jnp.where(is_first, v, zero) for v in (s, st)]
            shared += [jnp.where(is_second, v, zero) for v in (s, st)]
            shared = jnp.concatenate(shared, axis=0)
            edge = jnp.dot(shared, green(WINDOWS[4], 128), preferred_element_type=f32)
            one = jnp.dot(first, green(WINDOWS[0], 256), preferred_element_type=f32)
            two = jnp.dot(second, green(WINDOWS[2], 256), preferred_element_type=f32)
            total.append((one + edge[0:32], two + edge[32:64]))
        one, two = (p + q for p, q in zip(*total))
        x = (one[0:16], one[16:32], two[0:16], two[16:32])
        for yh in range(2):
            v = jnp.concatenate([g[8 * yh : 8 * yh + 8] for g in x], axis=0)
            out_ref[yh, i] = v.astype(bf16)

    @pl.loop(0, PAR // 16)
    def _(m):
        for u in range(16):
            pair(16 * m + u, pl.multiple_of(m * 9600, 16) + 600 * u)


def smooth_kernel(moved_ref, left_ref, put_ref, gather_ref, out_ref, both, grid, sol, coef_ref):
    coefficients(left_ref, put_ref, coef_ref)
    series = chebyshev_series()

    def start(b, _):
        v = moved_ref[b].astype(f32) + moved_ref[PAR + b].astype(f32)
        v = v.astype(bf16).astype(f32).reshape(4, 8, 128)
        grid[b] = v
        both[0, b + 1] = series[5] * v
        return 0

    lax.fori_loop(0, PAR, start, 0, unroll=UNROLL)

    def halo(slot):
        both[slot, 0] = pltpu.roll(both[slot, PAR], 1, 2)
        both[slot, PAR + 1] = pltpu.roll(both[slot, 1], 127, 2)

    for k in range(4, -1, -1):
        now, later = k % 2, (k + 1) % 2
        halo(now)

        def step(b, _, k=k, now=now, later=later):
            def coef(n):
                return coef_ref[n, b]

            u = both[now, b + 1]
            v = coef(0) * u
            v = v + coef(1) * pltpu.roll(u, 4, 2)
            v = v + coef(2) * pltpu.roll(u, 124, 2)
            v = v + coef(3) * both[now, b]
            v = v + coef(4) * both[now, b + 2]
            if k == 0:
                v = 0.5 * v
            v = v + series[k] * grid[b]
            if k < 4:
                v = v - both[later, b + 1]
            if k == 0:
                sol[pl.ds(pl.multiple_of(b * 32, 32), 32), :] = v.reshape(32, 128)
            else:
                both[later, b + 1] = v
            return 0

        lax.fori_loop(0, PAR, step, 0, unroll=UNROLL)
    quarter = iota((32, 128), 1) & 3
    for pair in (0, 16):
        turned = []
        for f in range(8):
            column = []
            for g in (pair, pair + 8):
                x = sol[pl.ds(g + f, 32, stride=32), :]
                column += [jnp.where(quarter == q, x, 0.0).astype(bf16) for q in range(4)]
            turned.append(jnp.concatenate(column, axis=0))
        turned = jnp.concatenate(turned, axis=1)
        y = lax.dot_general(gather_ref[...], turned, NT_DIMS, preferred_element_type=f32)
        for n, g in enumerate((pair, pair + 8)):
            v = y[:, n * 128 : (n + 1) * 128].reshape(ROWS, 8, 128)
            out_ref[:, g : g + 8, :] = v.astype(bf16)


def inverse_kernel(back_ref, itab_ref, out_hbm, wide, mixed, ready, sems):
    wide[...] = back_ref[...].reshape(PAR * 32, 128).astype(f32)
    xs = [wide[pl.ds(r, 128, stride=8), :].astype(bf16) for r in range(8)]
    copies = []
    for n, (start, count) in enumerate(((0, 144), (144, 144), (288, 132))):
        at = pl.ds(start, count)
        itab = itab_ref[at, :]
        for r in range(8):
            y = jnp.dot(itab, xs[r], preferred_element_type=f32)
            mixed[pl.ds(8 * start + r, count, stride=8), :] = y
        y = mixed[8 * start : 8 * (start + count), :].astype(bf16)
        ready[at] = y.reshape(count, 8, 128)
        copies.append(pltpu.make_async_copy(ready.at[at], out_hbm.at[at], sems.at[n]))
        copies[-1].start()
    for copy in copies:
        copy.wait()


def call(kernel, out, in_specs, scratch=(), mib=8, to=VMEM):
    many = isinstance(out, (tuple, list))
    return pl.pallas_call(
        kernel,
        out_shape=out,
        in_specs=in_specs,
        out_specs=[to] * len(out) if many else to,
        scratch_shapes=list(scratch),
        compiler_params=pltpu.CompilerParams(vmem_limit_bytes=mib << 20),
    )


def shape(*dims, dtype=bf16):
    return jax.ShapeDtypeStruct(dims, dtype)


def in_hbm(x):
    return pltpu.with_memory_space_constraint(x, pltpu.HBM)


def partner(bit):
    return [(s * PAR + b, (s ^ bit) * PAR + b) for s in range(SENS) for b in range(PAR)]


def local(data, green, freqs, sensor_order, kappa, theta):
    spectra = call(
        spectra_kernel,
        shape(PAD, 128),
        [HBM, HBM],
        [
            pltpu.VMEM((HERE, R, NT), bf16),
            pltpu.SMEM((K,), i32),
            pltpu.SemaphoreType.DMA((PIECES + 1,)),
        ],
        mib=52,
    )(in_hbm(freqs), in_hbm(jnp.transpose(data, (1, 0, 2))))
    table = green.reshape(K * HERE * 2, 128)
    order = sensor_order.reshape(1, HERE)
    far = lax.ppermute(spectra, AXES, partner(2))
    near = lax.ppermute(spectra, AXES, partner(1))
    here, itab, gather, put = call(
        fetch_kernel,
        [shape(K * HERE * 2, 128), shape(NT, 128), shape(256, 1024), shape(2, 1024, 128)],
        [HBM, VMEM],
        [pltpu.SemaphoreType.DMA((4,))],
    )(in_hbm(table), freqs.reshape(1, K))
    far, near, here, order = lax.optimization_barrier((far, near, here, order))
    order_two = lax.ppermute(order, AXES, partner(1))
    last = lax.ppermute(far, AXES, partner(1))
    last, order_two, here = lax.optimization_barrier((last, order_two, here))
    swapped = lax.ppermute(here, AXES, partner(1))
    sent = call(slots_kernel, shape(PAR, BLOCK, 128), [VMEM] * 8)(
        spectra, near, far, last, order, order_two, kappa, theta
    )
    left = lax.all_to_all(sent, "par", 0, 0, tiled=True)
    summed = call(
        product_kernel,
        shape(2, PAR, 32, 128),
        [VMEM] * 3,
        [
            pltpu.VMEM((PAR, BLOCK, 128), bf16),
        ],
    )(left, here, swapped).reshape(2 * PAR, 32, 128)
    groups = [[(2 * y + c) * PAR + b for y in range(2) for b in range(PAR)] for c in range(2)]
    moved = lax.all_to_all(summed, AXES, 0, 0, tiled=True, axis_index_groups=groups)
    smooth = call(
        smooth_kernel,
        shape(ROWS, 32, 128),
        [VMEM] * 4,
        [
            pltpu.VMEM((2, PAR + 2, 4, 8, 128), f32),
            pltpu.VMEM((PAR, 4, 8, 128), f32),
            pltpu.VMEM((PAR * 32, 128), f32),
            pltpu.VMEM((5, 32, 8, 128), f32),
        ],
    )(moved, left, put, gather)
    back = lax.all_to_all(smooth, "par", 0, 0, tiled=True)
    out = call(
        inverse_kernel,
        shape(NT, 8, 128),
        [VMEM, VMEM],
        [
            pltpu.VMEM((PAR * 32, 128), f32),
            pltpu.VMEM((NT * 8, 128), f32),
            pltpu.VMEM((NT, 8, 128), bf16),
            pltpu.SemaphoreType.DMA((3,)),
        ],
        to=HBM,
    )(back, itab)
    return jnp.transpose(out, (1, 0, 2)).reshape(8, NT, 1, 128)


def solution(mesh):
    placed = (
        P(None, "sens", None),
        P(None, "sens", None, "par"),
        P(),
        P("sens"),
        P("par", None),
        P("par", None),
    )
    return jax.shard_map(
        local, mesh=mesh, in_specs=placed, out_specs=P("sens", None, "par", None), check_vma=False
    )
```

```python
import math

import jax
import jax.numpy as jnp
from jax import lax
from jax.experimental import pallas as pl
from jax.experimental.pallas import tpu as pltpu
from jax.sharding import PartitionSpec as P

NT = 420
K = 64
R = 32
ROWS = 32
SWEEPS = 6
SENS = 4
PAR = 32
HERE = 150
PAD = 160
TIMES = 432
WINDOWS = (0, 128, 344, 472, 256)
BLOCK = 32 * len(WINDOWS)
CHUNK = 80
UNROLL = 16
PIECES = -(-HERE // CHUNK)
AXES = ("sens", "par")
LOWER, UPPER = 0.05, 16.5
f32, bf16, i32 = jnp.float32, jnp.bfloat16, jnp.int32
VMEM = pl.BlockSpec(memory_space=pltpu.VMEM)
SMEM = pl.BlockSpec(memory_space=pltpu.SMEM)
HBM = pl.BlockSpec(memory_space=pltpu.HBM)
NT_DIMS = (((1,), (1,)), ((), ()))
TN_DIMS = (((0,), (0,)), ((), ()))


def iota(shape, dim):
    return lax.broadcasted_iota(i32, shape, dim)


def chebyshev_series():
    d, c = 0.5 * (UPPER + LOWER), 0.5 * (UPPER - LOWER)
    values = []
    for m in range(SWEEPS):
        lam = d - c * math.cos(math.pi * (m + 0.5) / SWEEPS)
        x, res, dirn, alpha = 0.0, 1.0, 0.0, 1.0 / d
        for i in range(SWEEPS):
            beta = 0.0
            if i > 0:
                beta = 0.5 * (c * alpha) ** 2 if i == 1 else (c * alpha / 2.0) ** 2
                alpha = 1.0 / (d - beta / alpha)
            dirn = res + beta * dirn
            x = x + alpha * dirn
            res = res - alpha * lam * dirn
        values.append(x)
    series = [
        2.0 / SWEEPS * sum(v * math.cos(k * math.pi * (m + 0.5) / SWEEPS) for m, v in enumerate(values))
        for k in range(SWEEPS)
    ]
    return [0.5 * series[0]] + series[1:]


def wave(freq, imag, shape, dim):
    t = iota(shape, dim).astype(f32)
    p = t * freq
    m = p - NT * jnp.floor(p * (1.0 / NT))
    m = jnp.where(m < 0, m + NT, m)
    m = jnp.where(m >= NT, m - NT, m)
    m = jnp.where(imag, m + NT // 4, m)
    m = jnp.where(m >= NT, m - NT, m)
    x = (NT // 4 - jnp.minimum(m, NT - m)) * (2.0 * math.pi / NT)
    x2 = x * x
    acc = -1.0 / math.factorial(11) + x2 * (1.0 / math.factorial(13))
    for n, sign in ((9, 1), (7, -1), (5, 1), (3, -1)):
        acc = sign / math.factorial(n) + x2 * acc
    return x + x * x2 * acc


def spectra_kernel(freqs_hbm, data_ref, out_ref, buf, freqs_ref, sems):
    freqs_copy = pltpu.make_async_copy(freqs_hbm, freqs_ref, sems.at[PIECES])
    freqs_copy.start()
    copies = []
    for n in range(PIECES):
        at = pl.ds(n * CHUNK, min(CHUNK, HERE - n * CHUNK))
        copies.append(pltpu.make_async_copy(data_ref.at[at], buf.at[at], sems.at[n]))
        copies[-1].start()
    freqs_copy.wait()
    first = 2 * lax.axis_index("par")
    line = iota((8, NT), 0)
    freq = jnp.where(line < 2, freqs_ref[first], freqs_ref[first + 1]).astype(f32)
    table = wave(freq, (line & 1) == 1, (8, NT), 1) * (1.0 / math.sqrt(NT))
    table = [jnp.broadcast_to(table[j : j + 1], (R, NT)) for j in range(4)]
    table = jnp.concatenate(table, axis=0).astype(bf16)
    own = (iota((R, 128), 1) & 31) == iota((R, 128), 0)
    own = jnp.where(own, 1.0, 0.0).astype(f32).reshape(1, 4, 8, 128)
    fold = (iota((CHUNK, CHUNK * 8), 1) >> 3) == iota((CHUNK, CHUNK * 8), 0)
    fold = jnp.where(fold, 1.0, 0.0).astype(bf16)
    for n, copy in enumerate(copies):
        copy.wait()
        count = min(CHUNK, HERE - n * CHUNK)
        parts = []
        for start in range(0, count, count // 2):
            at = n * CHUNK + start
            x = buf[at : at + count // 2].reshape(count // 2 * R, NT)
            y = lax.dot_general(x, table, NT_DIMS, preferred_element_type=f32)
            y = jnp.sum(y.reshape(count // 2, 4, 8, 128) * own, axis=1)
            parts.append(y.reshape(count // 2 * 8, 128))
        y = jnp.concatenate(parts, axis=0).astype(bf16)
        rows = -(-count // 16) * 16
        y = jnp.dot(fold[:rows, : count * 8], y, preferred_element_type=f32)
        out_ref[n * CHUNK : n * CHUNK + rows, :] = y.astype(bf16)


def split3(x):
    hi = x.astype(bf16).astype(f32)
    mid = (x - hi).astype(bf16).astype(f32)
    return hi, mid, x - hi - mid


def slots_kernel(
    own_ref, core_ref, far_ref, last_ref, order_ref, other_ref, kappa_ref, theta_ref, out_ref
):
    sens = lax.axis_index("sens")
    every = [ref[...] for ref in (own_ref, core_ref, far_ref, last_ref)]
    every = jnp.concatenate(every, axis=0)
    width = 128 * len(WINDOWS)
    at = iota((HERE, width), 1)
    green_row = at
    for n, start in enumerate(WINDOWS):
        green_row = jnp.where((at >> 7) == n, start + (at & 127), green_row)
    slot = jnp.where(green_row >= 2 * HERE, green_row - 2 * HERE, green_row) >> 1
    shared_end = (at >= 4 * 128) & ((at & 127) >= WINDOWS[2] - WINDOWS[4])
    slot = jnp.where(shared_end, -1, slot)
    spread = jnp.where(slot == iota((HERE, width), 0), 1.0, 0.0).astype(bf16)
    lane = iota((R, 128), 1)
    odd = (lane & 1) == 1

    def windows(order):
        block = jnp.where(order >= 150, 1, 0)
        block = jnp.where(order >= 300, 2, block)
        block = jnp.where(order >= 450, 3, block)
        row = (block ^ sens) * PAD + order - HERE * block
        pick = jnp.where(iota((SENS * PAD, HERE), 0) == row, 1.0, 0.0).astype(bf16)
        chosen = lax.dot_general(every, pick, TN_DIMS, preferred_element_type=f32)
        wide = jnp.dot(chosen.astype(bf16), spread, preferred_element_type=f32)
        for n in range(len(WINDOWS)):
            w = wide[:, n * 128 : (n + 1) * 128]
            first = jnp.where(odd, w[32:64], w[0:32])
            second = jnp.where(odd, w[96:128], w[64:96])
            if n < 2:
                v = first
            elif n < 4:
                v = second
            else:
                v = jnp.where(lane < 2 * HERE - WINDOWS[4], first, second)
            zero = (sens & 1) == 0
            yield [jnp.where(zero, v[y : y + 8], v[y + 8 : y + 16]) for y in (0, 16)]

    parts = jnp.zeros((8, 128), f32)
    for n, v in enumerate(split3(kappa_ref[...]) + split3(theta_ref[...])):
        parts = jnp.where(iota((8, 128), 0) == n, v, parts)
    turns = [parts if q == 3 else pltpu.roll(parts, 96 - 32 * q, 1) for q in range(4)]
    rows = []
    for one, two in zip(windows(order_ref[...]), windows(other_ref[...])):
        rows += one + two
    low = iota((8, 128), 1) < 96
    for q in range(4):
        rows[16 + q] = jnp.where(low, rows[16 + q], turns[q])
    block_out = jnp.concatenate(rows, axis=0).astype(bf16)
    for n in range(PAR):
        out_ref[n] = block_out


def coefficients(left_ref, coef_ref):
    flat = left_ref[:, BLOCK - 32 :, :].reshape(PAR * 32, 128)
    lane = iota((32, 128), 1)
    cell = iota((32, 128), 0)
    pick = jnp.where(lane == 96 + cell, 1.0, 0.0).astype(bf16)
    turned = lax.dot_general(pick, flat, NT_DIMS, preferred_element_type=f32).astype(bf16)
    row, to = iota((PAR * 32, 128), 0), iota((PAR * 32, 128), 1)
    here = to == 4 * (row >> 5) + ((row >> 3) & 3)
    part = row & 7
    put = jnp.where(here & (part < 3), 1.0, 0.0).astype(bf16)
    kappa = jnp.dot(turned, put, preferred_element_type=f32)
    put = jnp.where(here & (part >= 3) & (part < 6), 1.0, 0.0).astype(bf16)
    theta = jnp.dot(turned, put, preferred_element_type=f32)
    up, down = lane < 4, lane >= 124
    left = (cell == 0) & ((lane & 3) == 0)
    right = (cell == 31) & ((lane & 3) == 3)
    north = jnp.where(up, theta, pltpu.roll(theta, 4, 1))
    south = jnp.where(down, theta, pltpu.roll(theta, 124, 1))
    back = pltpu.roll(theta, 1, 0)
    west = jnp.where(cell == 0, pltpu.roll(back, 1, 1), back)
    west = jnp.where(left, theta, west)
    ahead = pltpu.roll(theta, 31, 0)
    east = jnp.where(cell == 31, pltpu.roll(ahead, 127, 1), ahead)
    east = jnp.where(right, theta, east)
    north, south, west, east = (0.5 * (theta + v) for v in (north, south, west, east))
    d, c = 0.5 * (UPPER + LOWER), 0.5 * (UPPER - LOWER)
    coefs = [
        (2.0 / c) * (d - (kappa + north + south + west + east)),
        jnp.where(up, 0.0, (2.0 / c) * north),
        jnp.where(down, 0.0, (2.0 / c) * south),
        jnp.where(left, 0.0, (2.0 / c) * west),
        jnp.where(right, 0.0, (2.0 / c) * east),
    ]
    for n, v in enumerate(coefs):
        coef_ref[n] = jnp.broadcast_to(v.reshape(32, 1, 128), (32, 8, 128))


def tables(freqs_ref, itab_ref, gather_ref):
    m, n = iota((256, 1024), 0), iota((256, 1024), 1)
    same = ((m & 7) == (n >> 7)) & ((m >> 3) == ((n & 127) >> 2))
    gather_ref[...] = jnp.where(same, 1.0, 0.0).astype(bf16)
    twice = jnp.where((iota((K, 128), 1) >> 1) == iota((K, 128), 0), 1.0, 0.0).astype(bf16)
    freqs = jnp.broadcast_to(freqs_ref[...].astype(f32), (8, K)).astype(bf16)
    freq = jnp.dot(freqs, twice, preferred_element_type=f32)[0:1]
    imag = (iota((TIMES, 128), 1) & 1) == 1
    itab_ref[...] = (wave(freq, imag, (TIMES, 128), 0) * (1.0 / math.sqrt(K))).astype(bf16)


def fetch_kernel(green_hbm, freqs_ref, out_ref, itab_ref, gather_ref, sems):
    rows = K * HERE * 2 // 4
    copies = []
    for n in range(4):
        at = pl.ds(n * rows, rows)
        copies.append(pltpu.make_async_copy(green_hbm.at[at], out_ref.at[at], sems.at[n]))
        copies[-1].start()
    tables(freqs_ref, itab_ref, gather_ref)
    for copy in copies:
        copy.wait()


def product_kernel(left_ref, green_ref, swapped_ref, out_ref, turned_ref):
    a, b = iota((128, 128), 0), iota((128, 128), 1)
    turn = jnp.where((a ^ 1) == b, jnp.where((a & 1) == 1, 1.0, -1.0), 0.0).astype(bf16)
    lane = iota((16, 128), 1)
    is_first = lane < 2 * HERE - WINDOWS[4]
    is_second = (lane >= 2 * HERE - WINDOWS[4]) & (lane < WINDOWS[2] - WINDOWS[4])
    zero = jnp.zeros((16, 128), bf16)

    @pl.loop(0, PAR // 8)
    def _(m):
        x = left_ref[pl.ds(8 * m, 8)].reshape(8 * BLOCK, 128)
        x = jnp.dot(x, turn, preferred_element_type=f32).astype(bf16)
        turned_ref[pl.ds(8 * m, 8)] = x.reshape(8, BLOCK, 128)

    def pair(i, base):
        total = []
        for half, green_of in enumerate((green_ref, swapped_ref)):

            def part(n, ref):
                return ref[i, n * 32 + half * 16 : n * 32 + half * 16 + 16, :]

            def both(n, ref):
                return jnp.concatenate([part(n, ref), part(n + 1, ref)], axis=1)

            def green(start, count):
                return green_of[pl.ds(base + start, count), :]

            first = jnp.concatenate([both(0, left_ref), both(0, turned_ref)], axis=0)
            second = jnp.concatenate([both(2, left_ref), both(2, turned_ref)], axis=0)
            s, st = part(4, left_ref), part(4, turned_ref)
            shared = [jnp.where(is_first, v, zero) for v in (s, st)]
            shared += [jnp.where(is_second, v, zero) for v in (s, st)]
            shared = jnp.concatenate(shared, axis=0)
            edge = jnp.dot(shared, green(WINDOWS[4], 128), preferred_element_type=f32)
            one = jnp.dot(first, green(WINDOWS[0], 256), preferred_element_type=f32)
            two = jnp.dot(second, green(WINDOWS[2], 256), preferred_element_type=f32)
            total.append((one + edge[0:32], two + edge[32:64]))
        one, two = (p + q for p, q in zip(*total))
        x = (one[0:16], one[16:32], two[0:16], two[16:32])
        for yh in range(2):
            v = jnp.concatenate([g[8 * yh : 8 * yh + 8] for g in x], axis=0)
            out_ref[yh, i] = v.astype(bf16)

    @pl.loop(0, PAR // 16)
    def _(m):
        for u in range(16):
            pair(16 * m + u, pl.multiple_of(m * 9600, 16) + 600 * u)


def smooth_kernel(moved_ref, left_ref, gather_ref, out_ref, both, grid, sol, coef_ref):
    coefficients(left_ref, coef_ref)
    series = chebyshev_series()

    def start(b, _):
        v = moved_ref[b].astype(f32) + moved_ref[PAR + b].astype(f32)
        v = v.astype(bf16).astype(f32).reshape(4, 8, 128)
        grid[b] = v
        both[0, b + 1] = series[5] * v
        return 0

    lax.fori_loop(0, PAR, start, 0, unroll=UNROLL)

    def halo(slot):
        both[slot, 0] = pltpu.roll(both[slot, PAR], 1, 2)
        both[slot, PAR + 1] = pltpu.roll(both[slot, 1], 127, 2)

    for k in range(4, -1, -1):
        now, later = k % 2, (k + 1) % 2
        halo(now)

        def step(b, _, k=k, now=now, later=later):
            def coef(n):
                return coef_ref[n, b]

            u = both[now, b + 1]
            v = coef(0) * u
            v = v + coef(1) * pltpu.roll(u, 4, 2)
            v = v + coef(2) * pltpu.roll(u, 124, 2)
            v = v + coef(3) * both[now, b]
            v = v + coef(4) * both[now, b + 2]
            if k == 0:
                v = 0.5 * v
            v = v + series[k] * grid[b]
            if k < 4:
                v = v - both[later, b + 1]
            if k == 0:
                sol[pl.ds(pl.multiple_of(b * 32, 32), 32), :] = v.reshape(32, 128)
            else:
                both[later, b + 1] = v
            return 0

        lax.fori_loop(0, PAR, step, 0, unroll=UNROLL)
    quarter = iota((32, 128), 1) & 3
    for pair in (0, 16):
        turned = []
        for f in range(8):
            column = []
            for g in (pair, pair + 8):
                x = sol[pl.ds(g + f, 32, stride=32), :]
                column += [jnp.where(quarter == q, x, 0.0).astype(bf16) for q in range(4)]
            turned.append(jnp.concatenate(column, axis=0))
        turned = jnp.concatenate(turned, axis=1)
        y = lax.dot_general(gather_ref[...], turned, NT_DIMS, preferred_element_type=f32)
        for n, g in enumerate((pair, pair + 8)):
            v = y[:, n * 128 : (n + 1) * 128].reshape(ROWS, 8, 128)
            out_ref[:, g : g + 8, :] = v.astype(bf16)


def inverse_kernel(back_ref, itab_ref, out_hbm, wide, mixed, ready, sems):
    wide[...] = back_ref[...].reshape(PAR * 32, 128).astype(f32)
    xs = [wide[pl.ds(r, 128, stride=8), :].astype(bf16) for r in range(8)]
    copies = []
    step = TIMES // 3
    for n in range(3):
        at = pl.ds(n * step, step)
        itab = itab_ref[at, :]
        for r in range(8):
            y = jnp.dot(itab, xs[r], preferred_element_type=f32)
            mixed[pl.ds(8 * n * step + r, step, stride=8), :] = y
        y = mixed[8 * n * step : 8 * (n + 1) * step, :].astype(bf16)
        ready[at] = y.reshape(step, 8, 128)
        used = pl.ds(n * step, min(step, NT - n * step))
        copies.append(pltpu.make_async_copy(ready.at[used], out_hbm.at[used], sems.at[n]))
        copies[-1].start()
    for copy in copies:
        copy.wait()


def call(kernel, out, in_specs, scratch=(), mib=8, to=VMEM):
    many = isinstance(out, (tuple, list))
    return pl.pallas_call(
        kernel,
        out_shape=out,
        in_specs=in_specs,
        out_specs=[to] * len(out) if many else to,
        scratch_shapes=list(scratch),
        compiler_params=pltpu.CompilerParams(vmem_limit_bytes=mib << 20),
    )


def shape(*dims, dtype=bf16):
    return jax.ShapeDtypeStruct(dims, dtype)


def in_hbm(x):
    return pltpu.with_memory_space_constraint(x, pltpu.HBM)


def partner(bit):
    return [(s * PAR + b, (s ^ bit) * PAR + b) for s in range(SENS) for b in range(PAR)]


def local(data, green, freqs, sensor_order, kappa, theta):
    spectra = call(
        spectra_kernel,
        shape(PAD, 128),
        [HBM, HBM],
        [
            pltpu.VMEM((HERE, R, NT), bf16),
            pltpu.SMEM((K,), i32),
            pltpu.SemaphoreType.DMA((PIECES + 1,)),
        ],
        mib=52,
    )(in_hbm(freqs), in_hbm(jnp.transpose(data, (1, 0, 2))))
    table = green.reshape(K * HERE * 2, 128)
    order = sensor_order.reshape(1, HERE)
    far = lax.ppermute(spectra, AXES, partner(2))
    near = lax.ppermute(spectra, AXES, partner(1))
    here, itab, gather = call(
        fetch_kernel,
        [shape(K * HERE * 2, 128), shape(TIMES, 128), shape(256, 1024)],
        [HBM, VMEM],
        [pltpu.SemaphoreType.DMA((4,))],
    )(in_hbm(table), freqs.reshape(1, K))
    far, near, here, order = lax.optimization_barrier((far, near, here, order))
    order_two = lax.ppermute(order, AXES, partner(1))
    last = lax.ppermute(far, AXES, partner(1))
    last, order_two, here = lax.optimization_barrier((last, order_two, here))
    swapped = lax.ppermute(here, AXES, partner(1))
    sent = call(slots_kernel, shape(PAR, BLOCK, 128), [VMEM] * 8)(
        spectra, near, far, last, order, order_two, kappa, theta
    )
    left = lax.all_to_all(sent, "par", 0, 0, tiled=True)
    summed = call(
        product_kernel,
        shape(2, PAR, 32, 128),
        [VMEM] * 3,
        [
            pltpu.VMEM((PAR, BLOCK, 128), bf16),
        ],
    )(left, here, swapped).reshape(2 * PAR, 32, 128)
    groups = [[(2 * y + c) * PAR + b for y in range(2) for b in range(PAR)] for c in range(2)]
    moved = lax.all_to_all(summed, AXES, 0, 0, tiled=True, axis_index_groups=groups)
    smooth = call(
        smooth_kernel,
        shape(ROWS, 32, 128),
        [VMEM] * 3,
        [
            pltpu.VMEM((2, PAR + 2, 4, 8, 128), f32),
            pltpu.VMEM((PAR, 4, 8, 128), f32),
            pltpu.VMEM((PAR * 32, 128), f32),
            pltpu.VMEM((5, 32, 8, 128), f32),
        ],
    )(moved, left, gather)
    back = lax.all_to_all(smooth, "par", 0, 0, tiled=True)
    out = call(
        inverse_kernel,
        shape(NT, 8, 128),
        [VMEM, VMEM],
        [
            pltpu.VMEM((PAR * 32, 128), f32),
            pltpu.VMEM((TIMES * 8, 128), f32),
            pltpu.VMEM((TIMES, 8, 128), bf16),
            pltpu.SemaphoreType.DMA((3,)),
        ],
        to=HBM,
    )(back, itab)
    return jnp.transpose(out, (1, 0, 2)).reshape(8, NT, 1, 128)


def solution(mesh):
    placed = (
        P(None, "sens", None),
        P(None, "sens", None, "par"),
        P(),
        P("sens"),
        P("par", None),
        P("par", None),
    )
    return jax.shard_map(
        local, mesh=mesh, in_specs=placed, out_specs=P("sens", None, "par", None), check_vma=False
    )
```
